32 devices in a mesh: group: 2 (over y), seq: 4 (over z), req: 2 (over x), sub: 2 (over core).
Axes of the slice: x: 2, y: 2, z: 4, core: 2. Of those that a mesh axis runs over, the one named last changes fastest.
Arguments:
- latent_codes: bfloat16 [2, 16, 2048, 512], P(None, ('group', 'req', 'sub'), 'seq'), parts along dimension 1, may hold values from -6 to 6
- latent_scales: bfloat16 [2, 16, 2048, 4], P(None, ('group', 'req', 'sub'), 'seq'), parts along dimension 1, may hold values from 0.34 to 3.5
- rope_keys: bfloat16 [2, 16, 2048, 64], P(None, ('group', 'req', 'sub'), 'seq'), parts along dimension 1, may hold values from -6 to 6
- lengths: int32 [16], P(('group', 'req', 'sub')), parts along dimension 0, may hold values from 256 to 2048, as said below
- query_latent: bfloat16 [2, 16, 4, 128, 512], P(None, ('group', 'req', 'sub'), None, 'seq'), parts along dimension 1, may hold values from -64 to 64
- query_rope: bfloat16 [2, 16, 4, 128, 64], P(None, ('group', 'req', 'sub'), None, 'seq'), parts along dimension 1, may hold values from -8 to 8
- new_latent: bfloat16 [2, 16, 4, 512], P(None, ('group', 'req', 'sub')), parts along dimension 1, may hold values from -9 to 9
- new_rope: bfloat16 [2, 16, 4, 64], P(None, ('group', 'req', 'sub')), parts along dimension 1, may hold values from -6 to 6
Outputs:
- attended: bfloat16 [2, 16, 4, 128, 512], P(None, ('group', 'req', 'sub'), None, 'seq'), parts along dimension 1
- cache_codes: bfloat16 [2, 16, 512, 4, 512], P(None, ('group', 'req', 'sub'), None, 'seq'), parts along dimension 1
- cache_scales: bfloat16 [2, 16, 512, 4, 4], P(None, ('group', 'req', 'sub'), None, 'seq'), parts along dimension 1
- cache_rope: bfloat16 [2, 16, 512, 4, 64], P(None, ('group', 'req', 'sub'), None, 'seq'), parts along dimension 1
The draws below stay inside these ranges and needn't reach their ends.
There are 2 independent parts, one for each index of `group`. The reference program is written for one: setup_inputs(seed, part) draws one part's arguments, and reference() takes and returns one part's arrays. A program takes and returns all parts, laid end to end along the dimension named above; each array names one. Nothing has to cross between parts.
Inputs may be any that keep to these rules, and one draw needn't show every extreme that they name: `lengths`: one request is exactly 2048 long.
All inputs are finite; a program needn't handle non-finite values.
Results may differ from the reference program's by a relative error of at most 0.013.
Values may be sent and summed in bfloat16 or wider, within the bound.
A program may use at most 64 MiB of HBM per device.

```python
import jax
import jax.numpy as jnp
from jax import lax

LAT = 512
ROPE = 64
HEADS = 128
BLK = 128
LAYERS = 2
DEC = 4
REQS = 8
S_MAX = 2048
N_SEQ = 4


def head_positions(key):
    codes_head = jax.random.normal(jax.random.fold_in(key, 101), (LAYERS, REQS, 2, LAT), jnp.float32)
    codes_head = jnp.clip(codes_head, -6.0, 6.0)
    scales_head = jnp.exp(jax.random.uniform(jax.random.fold_in(key, 103), (LAYERS, REQS, 2, LAT // BLK), jnp.float32, jnp.log(0.35), jnp.log(3.5)))
    return (codes_head, scales_head)


def new_keys_of(key):
    values = 1.5 * jax.random.normal(jax.random.fold_in(key, 106), (LAYERS, REQS, DEC, LAT), jnp.float32)
    return jnp.clip(values, -9.0, 9.0)


def draw_latent_codes(key, part):
    codes_head, scales_head = head_positions(key)
    rest = jax.random.normal(jax.random.fold_in(key, 104), (LAYERS, REQS, S_MAX - 2, LAT), jnp.float32)
    whole = jnp.concatenate([codes_head, jnp.clip(rest, -6.0, 6.0)], axis=2)
    return whole.astype(jnp.bfloat16)


def draw_latent_scales(key, part):
    codes_head, scales_head = head_positions(key)
    rest = jnp.exp(jax.random.uniform(jax.random.fold_in(key, 105), (LAYERS, REQS, S_MAX - 2, LAT // BLK), jnp.float32, jnp.log(0.35), jnp.log(3.5)))
    whole = jnp.concatenate([scales_head, rest], axis=2)
    return jnp.clip(whole, 0.35, 3.5).astype(jnp.bfloat16)


def draw_new_latent(key, part):
    return new_keys_of(key).astype(jnp.bfloat16)


def draw_query_latent(key, part):
    noise = 1.3 * jax.random.normal(jax.random.fold_in(key, 107), (LAYERS, REQS, DEC, HEADS, LAT), jnp.float32)
    values = noise + 0.2 * new_keys_of(key)[:, :, :, None, :]
    return jnp.clip(values, -64.0, 64.0).astype(jnp.bfloat16)


def draw_lengths(key, part):
    values = jax.random.randint(jax.random.fold_in(key, 109), (REQS,), S_MAX // 8, S_MAX + 1)
    longest = jax.random.randint(jax.random.fold_in(key, 110), (), 0, REQS)
    return jnp.where(jnp.arange(REQS, dtype=jnp.int32) == longest, S_MAX, values).astype(jnp.int32)


def levels(key, shape, cuts, smallest, high):
    def one(dim, shards_of):
        draws = jax.random.uniform(jax.random.fold_in(jax.random.fold_in(key, 6), dim), (shards_of,), jnp.float32, smallest / len(cuts), high / len(cuts))
        return jnp.repeat(jnp.exp(draws), shape[dim] // shards_of).reshape((-1,) + (1,) * (len(shape) - dim - 1))

    gain = one(*cuts[0])
    for cut in cuts[1:]:
        gain = gain * one(*cut)
    return gain


def normal_values(key, dims, spread, reach, cuts=(), held_as=jnp.bfloat16):
    result = jax.random.normal(key, dims, jnp.float32) * spread
    if len(cuts) > 0:
        result = levels(key, dims, cuts, -0.22, 0.18) * result
    return jnp.clip(result, min=-reach, max=reach).astype(held_as)


def setup_inputs(seed: int = 0, part: int = 0) -> dict:
    streams_of = jax.random.split(jax.random.key(seed), 9)
    part_keys = jax.random.split(jax.random.fold_in(streams_of[8], part), 9)
    return {
        "latent_codes": draw_latent_codes(jax.random.fold_in(jax.random.fold_in(streams_of[8], part), 71), part),
        "latent_scales": draw_latent_scales(jax.random.fold_in(jax.random.fold_in(streams_of[8], part), 71), part),
        "rope_keys": normal_values(part_keys[2], (LAYERS, REQS, S_MAX, ROPE), 1.0, 6.0, ((1, 4), (2, 4))),
        "lengths": draw_lengths(jax.random.fold_in(jax.random.fold_in(streams_of[8], part), 71), part),
        "query_latent": draw_query_latent(jax.random.fold_in(jax.random.fold_in(streams_of[8], part), 71), part),
        "query_rope": normal_values(part_keys[5], (LAYERS, REQS, DEC, HEADS, ROPE), 1.3, 8.0, ((1, 4), (3, 4))),
        "new_latent": draw_new_latent(jax.random.fold_in(jax.random.fold_in(streams_of[8], part), 71), part),
        "new_rope": normal_values(part_keys[7], (LAYERS, REQS, DEC, ROPE), 1.0, 6.0, ((1, 4),)),
    }


softmax_gain = 192.0 ** -0.5
masked_score = -1.0e30


def dequantize(code_values, scale_values):
    blocks = scale_values.shape[-1]
    latent_width = code_values.shape[-1]
    shaped = code_values.astype(jnp.float32).reshape(code_values.shape[:-1] + (blocks, latent_width // blocks))
    scaled = shaped * scale_values.astype(jnp.float32)[..., None]
    return scaled.reshape(code_values.shape).astype(jnp.bfloat16)


def shard_partial(lat_query, rope_query, key_rows, rope_rows, usable, new_keys, new_rope_rows, holds_new):
    tokens_new, head_count, latent_width = lat_query.shape
    query_rows = lat_query.reshape(tokens_new * head_count, latent_width)
    query_pos = rope_query.reshape(tokens_new * head_count, rope_query.shape[-1])
    scores = jnp.dot(query_rows, key_rows.T, preferred_element_type=jnp.float32)
    scores = (scores + jnp.dot(query_pos, rope_rows.T, preferred_element_type=jnp.float32)) * softmax_gain
    fresh_scores = jnp.dot(query_rows, new_keys.T, preferred_element_type=jnp.float32)
    fresh_scores = (fresh_scores + jnp.dot(query_pos, new_rope_rows.T, preferred_element_type=jnp.float32)) * softmax_gain
    token_of_row = jnp.arange(tokens_new * head_count, dtype=jnp.int32) // head_count
    causal = (jnp.arange(tokens_new, dtype=jnp.int32)[None, :] <= token_of_row[:, None]) & holds_new
    scores = jnp.where(usable[None, :], scores, masked_score)
    fresh_scores = jnp.where(causal, fresh_scores, masked_score)
    group_peak = jnp.maximum(jnp.max(scores, 1), jnp.max(fresh_scores, 1)).astype(jnp.bfloat16)
    peak_float = group_peak.astype(jnp.float32)[:, None]
    weights = jnp.where(usable[None, :], jnp.exp(scores - peak_float), 0.0).astype(jnp.bfloat16)
    fresh_weights = jnp.where(causal, jnp.exp(fresh_scores - peak_float), 0.0).astype(jnp.bfloat16)
    group_total = jnp.sum(weights.astype(jnp.float32), 1) + jnp.sum(fresh_weights.astype(jnp.float32), 1)
    group_sum = jnp.dot(weights, key_rows, preferred_element_type=jnp.float32)
    group_sum = group_sum + jnp.dot(fresh_weights, new_keys, preferred_element_type=jnp.float32)
    return (group_sum.astype(jnp.bfloat16).reshape(tokens_new, head_count, latent_width),
            group_peak.reshape(tokens_new, head_count),
            group_total.astype(jnp.bfloat16).reshape(tokens_new, head_count))


def merge_groups(pieces):
    group_sum, group_peak, group_total = pieces
    peak_float = group_peak.astype(jnp.float32)
    overall = jnp.max(peak_float, 0)
    factor = jnp.exp(peak_float - overall)
    numerator = jnp.sum(factor[..., None] * group_sum.astype(jnp.float32), 0)
    denominator = jnp.sum(factor * group_total.astype(jnp.float32), 0)
    return (numerator / denominator[..., None]).astype(jnp.bfloat16)


def reference(latent_codes, latent_scales, rope_keys, lengths, query_latent, query_rope, new_latent, new_rope):
    shard_count = N_SEQ
    layer_count, request_count, full_length, latent_width = latent_codes.shape
    span = full_length // shard_count

    def regroup_rows(values):
        return values.reshape(layer_count, request_count, span, shard_count, values.shape[-1])

    cache_codes = regroup_rows(latent_codes)
    cache_scales = regroup_rows(latent_scales)
    cache_rope = regroup_rows(rope_keys)
    pair_count = layer_count * request_count

    def flatten_pairs(values):
        return values.reshape((pair_count,) + values.shape[2:])

    pair_lengths = jnp.tile(lengths, layer_count)
    groups = jnp.arange(shard_count, dtype=jnp.int32)
    offsets = jnp.arange(span, dtype=jnp.int32)
    positions = offsets[None, :] * shard_count + groups[:, None]
    holds_new = groups == 0

    def per_pair(inputs):
        codes_pair, scales_pair, rope_pair, length_pair, lat_query, rope_query, new_keys, new_rope_pair = inputs
        key_rows = jnp.swapaxes(dequantize(codes_pair, scales_pair), 0, 1)
        rope_rows = jnp.swapaxes(rope_pair, 0, 1)
        usable = positions < length_pair

        def per_group(group_inputs):
            key_group, rope_group, usable_group, holds_group = group_inputs
            return shard_partial(lat_query, rope_query, key_group, rope_group, usable_group, new_keys, new_rope_pair, holds_group)

        partial_sums = lax.map(per_group, (key_rows, rope_rows, usable, holds_new))
        return merge_groups(partial_sums)

    attended = lax.map(per_pair, (flatten_pairs(cache_codes), flatten_pairs(cache_scales), flatten_pairs(cache_rope),
                                  pair_lengths, flatten_pairs(query_latent), flatten_pairs(query_rope),
                                  flatten_pairs(new_latent), flatten_pairs(new_rope)))
    attended = attended.reshape(query_latent.shape)
    return (attended, cache_codes, cache_scales, cache_rope)
```

```python
import jax
import jax.numpy as jnp
from jax import lax
from jax.experimental import pallas as pl
from jax.experimental.pallas import tpu as pltpu
from jax.sharding import PartitionSpec as P

softmax_gain = 192.0 ** (-0.5)
masked_score = -1e30


def dequantize(code_values, scale_values):
    blocks = scale_values.shape[-1]
    latent_width = code_values.shape[-1]
    shaped = code_values.astype(jnp.float32).reshape(
        code_values.shape[:-1] + (blocks, latent_width // blocks)
    )
    scaled = shaped * scale_values.astype(jnp.float32)[..., None]
    return scaled.reshape(code_values.shape).astype(jnp.bfloat16)


def shard_partial(
    lat_query, rope_query, key_rows, rope_rows, usable, new_keys, new_rope_rows, holds_new
):
    tokens_new, head_count, latent_width = lat_query.shape
    query_rows = lat_query.reshape(tokens_new * head_count, latent_width)
    query_pos = rope_query.reshape(tokens_new * head_count, rope_query.shape[-1])
    scores = jnp.dot(query_rows, key_rows.T, preferred_element_type=jnp.float32)
    scores = (
        scores + jnp.dot(query_pos, rope_rows.T, preferred_element_type=jnp.float32)
    ) * softmax_gain
    fresh_scores = jnp.dot(query_rows, new_keys.T, preferred_element_type=jnp.float32)
    fresh_scores = (
        fresh_scores + jnp.dot(query_pos, new_rope_rows.T, preferred_element_type=jnp.float32)
    ) * softmax_gain
    token_of_row = jnp.arange(tokens_new * head_count, dtype=jnp.int32) // head_count
    causal = (jnp.arange(tokens_new, dtype=jnp.int32)[None, :] <= token_of_row[:, None]) & holds_new
    scores = jnp.where(usable[None, :], scores, masked_score)
    fresh_scores = jnp.where(causal, fresh_scores, masked_score)
    group_peak = jnp.maximum(jnp.max(scores, 1), jnp.max(fresh_scores, 1)).astype(jnp.bfloat16)
    peak_float = group_peak.astype(jnp.float32)[:, None]
    weights = jnp.where(usable[None, :], jnp.exp(scores - peak_float), 0.0).astype(jnp.bfloat16)
    fresh_weights = jnp.where(causal, jnp.exp(fresh_scores - peak_float), 0.0).astype(jnp.bfloat16)
    group_total = jnp.sum(weights.astype(jnp.float32), 1) + jnp.sum(
        fresh_weights.astype(jnp.float32), 1
    )
    group_sum = jnp.dot(weights, key_rows, preferred_element_type=jnp.float32)
    group_sum = group_sum + jnp.dot(fresh_weights, new_keys, preferred_element_type=jnp.float32)
    return (
        group_sum.astype(jnp.bfloat16).reshape(tokens_new, head_count, latent_width),
        group_peak.reshape(tokens_new, head_count),
        group_total.astype(jnp.bfloat16).reshape(tokens_new, head_count),
    )


def merge_groups(pieces):
    group_sum, group_peak, group_total = pieces
    peak_float = group_peak.astype(jnp.float32)
    overall = jnp.max(peak_float, 0)
    factor = jnp.exp(peak_float - overall)
    numerator = jnp.sum(factor[..., None] * group_sum.astype(jnp.float32), 0)
    denominator = jnp.sum(factor * group_total.astype(jnp.float32), 0)
    return (numerator / denominator[..., None]).astype(jnp.bfloat16)


def per_device(
    latent_codes, latent_scales, rope_keys, lengths, query_latent, query_rope, new_latent, new_rope
):
    shard_count = lax.axis_size("seq")
    seq_index = lax.axis_index("seq")
    layer_count, request_count, span, latent_width = latent_codes.shape
    lat_query, rope_query = (
        lax.all_gather(query_latent, "seq", axis=3, tiled=True),
        lax.all_gather(query_rope, "seq", axis=3, tiled=True),
    )

    def regroup_rows(values):
        return values.reshape(
            values.shape[0], values.shape[1], span // shard_count, shard_count, values.shape[-1]
        )

    codes_moved, scales_moved, rope_moved = (
        lax.all_to_all(regroup_rows(latent_codes), "seq", split_axis=3, concat_axis=2, tiled=True),
        lax.all_to_all(regroup_rows(latent_scales), "seq", split_axis=3, concat_axis=2, tiled=True),
        lax.all_to_all(regroup_rows(rope_keys), "seq", split_axis=3, concat_axis=2, tiled=True),
    )
    offsets = jnp.arange(span, dtype=jnp.int32)
    key_rows = dequantize(latent_codes, latent_scales)
    positions = seq_index * span + offsets
    usable = positions[None, :] < lengths[:, None]
    holds_new = seq_index == 0
    per_request = jax.vmap(shard_partial, in_axes=(0, 0, 0, 0, 0, 0, 0, None))
    per_layer = jax.vmap(per_request, in_axes=(0, 0, 0, 0, None, 0, 0, None))
    group_sum, group_peak, group_total = per_layer(
        lat_query, rope_query, key_rows, rope_keys, usable, new_latent, new_rope, holds_new
    )
    attended = merge_groups(
        (
            lax.all_to_all(group_sum[None], "seq", split_axis=4, concat_axis=0, tiled=True),
            lax.all_to_all(group_peak[None], "seq", split_axis=4, concat_axis=0, tiled=True),
            lax.all_to_all(group_total[None], "seq", split_axis=4, concat_axis=0, tiled=True),
        )
    )
    return (attended, codes_moved, scales_moved, rope_moved)


AUX = 80


def _relay_kernel(
    len_ref, codes_ref, aux_ref, q_ref, qr_ref, new_ref, newr_ref,
    att_ref, cache_ref, caux_ref,
    kbuf, abuf, qbuf, qrbuf, nkbuf, nrbuf, result, acc, peak, total,
    load_sem, out_sem, send_sem, recv_sem, q_send, q_recv, f_send, f_recv, r_send, r_recv,
):
    pairs, groups, rows, width = codes_ref.shape
    span = groups * rows
    half = q_ref.shape[1]
    rope = qr_ref.shape[2]
    heads = half // new_ref.shape[1]
    fresh = new_ref.shape[1]
    me = lax.axis_index("seq")
    inner = (me == 1) | (me == 2)
    outer = (me - 1) * 3
    across = 3 - me
    hub = 1 + me // 3

    def neighbour_signal(target):
        pl.semaphore_signal(
            pltpu.get_barrier_semaphore(), inc=1, device_id={"seq": target},
            device_id_type=pl.DeviceIdType.MESH,
        )

    loads = [
        pltpu.make_async_copy(codes_ref, kbuf.at[0], load_sem.at[0]),
        pltpu.make_async_copy(aux_ref, abuf.at[0], load_sem.at[1]),
        pltpu.make_async_copy(q_ref, qbuf.at[:, 0], load_sem.at[2]),
        pltpu.make_async_copy(qr_ref, qrbuf.at[:, 0], load_sem.at[3]),
    ]
    for load in loads:
        load.start()

    @pl.when(inner)
    def _():
        neighbour_signal(outer)
        neighbour_signal(across)
        pl.semaphore_wait(pltpu.get_barrier_semaphore(), 2)

    @pl.when(jnp.logical_not(inner))
    def _():
        neighbour_signal(hub)
        pl.semaphore_wait(pltpu.get_barrier_semaphore(), 1)

    def remote(src, dst, send, recv, target):
        return pltpu.make_async_remote_copy(
            src_ref=src, dst_ref=dst, send_sem=send, recv_sem=recv,
            device_id={"seq": target}, device_id_type=pl.DeviceIdType.MESH,
        )

    def shard(src_slot, dst_slot, c, target):
        return (
            remote(kbuf.at[src_slot, c], kbuf.at[dst_slot, c],
                   send_sem.at[0, dst_slot, c], recv_sem.at[0, dst_slot, c], target),
            remote(abuf.at[src_slot, c], abuf.at[dst_slot, c],
                   send_sem.at[1, dst_slot, c], recv_sem.at[1, dst_slot, c], target),
        )

    def queries(c, target):
        return (
            remote(qbuf.at[c, 0], qbuf.at[c, 1], q_send.at[0, c], q_recv.at[0, c], target),
            remote(qrbuf.at[c, 0], qrbuf.at[c, 1], q_send.at[1, c], q_recv.at[1, c], target),
        )

    def shard_of(slot, own, partner):
        base = own + (slot % 2) * (partner - own)
        return base + (slot // 2) * (3 - 2 * base)

    def handover(slot, c, group, place, target):
        return (
            remote(kbuf.at[slot, c, group], cache_ref.at[c, place],
                   f_send.at[0, slot, c], f_recv.at[0, slot, c], target),
            remote(abuf.at[slot, c, group], caux_ref.at[c, place],
                   f_send.at[1, slot, c], f_recv.at[1, slot, c], target),
        )

    def keep(slot, c, place):
        return (
            pltpu.make_async_copy(kbuf.at[slot, c, me], cache_ref.at[c, place], out_sem.at[0, slot, c]),
            pltpu.make_async_copy(abuf.at[slot, c, me], caux_ref.at[c, place], out_sem.at[1, slot, c]),
        )

    def results(c, target):
        return remote(result.at[c], att_ref.at[c], r_send.at[c], r_recv.at[c], target)

    def start(copies):
        for copy in copies:
            copy.start()

    for load in loads:
        load.wait()

    @pl.when(jnp.logical_not(inner))
    def _():
        @pl.loop(0, pairs)
        def _(c):
            copies = shard(0, 1, c, hub) + queries(c, hub)
            start(copies)
            start(keep(0, c, me))
            for copy in copies:
                copy.wait_send()

        @pl.loop(0, pairs)
        def _(c):
            for slot in (0, 2, 3):
                for copy in handover(slot, c, me, shard_of(slot, hub, me), hub):
                    copy.wait_recv()
            results(c, hub).wait_recv()
            for copy in keep(0, c, me):
                copy.wait()

    @pl.when(inner)
    def _():
        start(shard(0, 2, 0, across))
        start(shard(0, 2, 1, across))

        @pl.loop(0, pairs)
        def _(c):
            start(handover(0, c, outer, me, outer))
            start(keep(0, c, me))
            nkbuf[c] = jnp.zeros(nkbuf.shape[1:], nkbuf.dtype)
            nrbuf[c] = jnp.zeros(nrbuf.shape[1:], nrbuf.dtype)
            nkbuf[c, 0:fresh, :] = new_ref[c]
            nrbuf[c, 0:fresh, :] = newr_ref[c]

        def relay(c):
            for copy in shard(0, 1, c, outer):
                copy.wait_recv()
            start(shard(1, 3, c, across))
            start(keep(1, c, outer))

        relay(0)
        start(shard(0, 2, 2, across))

        @pl.loop(0, pairs)
        def _(c):
            @pl.when(c + 1 < pairs)
            def _():
                relay(c + 1)

            @pl.when(c + 3 < pairs)
            def _():
                start(shard(0, 2, c + 3, across))

            for copy in queries(c, outer):
                copy.wait_recv()
            q = qbuf[c].reshape(2 * half, width)
            qr = qrbuf[c].reshape(2 * half, rope)
            dims = (((1,), (1,)), ((), ()))
            s = lax.dot_general(q, nkbuf[c], dims, preferred_element_type=jnp.float32)
            s = s + lax.dot_general(qr, nrbuf[c], dims, preferred_element_type=jnp.float32)
            s = s * softmax_gain
            token = (lax.broadcasted_iota(jnp.int32, s.shape, 0) % half) // heads
            s = jnp.where(lax.broadcasted_iota(jnp.int32, s.shape, 1) <= token, s, masked_score)
            m = jnp.max(s, axis=1, keepdims=True)
            w = jnp.exp(s - m).astype(jnp.bfloat16)
            peak[...] = jnp.broadcast_to(m, peak.shape)
            total[...] = jnp.broadcast_to(
                jnp.sum(w.astype(jnp.float32), axis=1, keepdims=True), total.shape
            )
            acc[...] = jnp.dot(w, nkbuf[c], preferred_element_type=jnp.float32)
            length = len_ref[c % len_ref.shape[0]]

            @pl.loop(0, 4)
            def _(slot):
                place = shard_of(slot, me, outer)

                @pl.when(slot >= 2)
                def _():
                    for copy in shard(0, slot, c, across):
                        copy.wait_recv()
                    start(handover(slot, c, outer, place, outer))
                    start(keep(slot, c, place))

                keys, ropes = [], []
                for k in range(groups):
                    scales = abuf[slot, c, k, rope:AUX, :].astype(jnp.float32).T
                    codes = kbuf[slot, c, k].astype(jnp.float32)
                    blocks = [
                        codes[:, b * 128:(b + 1) * 128] * scales[:, b:b + 1]
                        for b in range(width // 128)
                    ]
                    keys.append(jnp.concatenate(blocks, axis=1).astype(jnp.bfloat16))
                    ropes.append(abuf[slot, c, k, 0:rope, :])
                keys = jnp.concatenate(keys, axis=0)
                q = qbuf[c].reshape(2 * half, width)
                qr = qrbuf[c].reshape(2 * half, rope)
                s = lax.dot_general(q, keys, dims, preferred_element_type=jnp.float32)
                s = s + jnp.dot(qr, jnp.concatenate(ropes, axis=1), preferred_element_type=jnp.float32)
                s = s * softmax_gain
                column = lax.broadcasted_iota(jnp.int32, (1, span), 1)
                position = place * span + (column % rows) * groups + column // rows
                s = jnp.where(position < length, s, masked_score)
                before = peak[:, 0:1]
                m = jnp.maximum(before, jnp.max(s, axis=1, keepdims=True))
                factor = jnp.exp(before - m)
                w = jnp.exp(s - m).astype(jnp.bfloat16)
                peak[...] = jnp.broadcast_to(m, peak.shape)
                total[...] = factor * total[...] + jnp.sum(w.astype(jnp.float32), axis=1, keepdims=True)
                acc[...] = factor * acc[...] + jnp.dot(w, keys, preferred_element_type=jnp.float32)

            done = (acc[...] / total[:, 0:1]).astype(jnp.bfloat16)
            result[c] = done[half:]
            results(c, outer).start()
            att_ref[c] = done[:half]

        @pl.loop(0, pairs)
        def _(c):
            for copy in shard(0, 2, c, across) + shard(1, 3, c, across):
                copy.wait_send()
            for slot in (0, 2, 3):
                for copy in handover(slot, c, outer, shard_of(slot, me, outer), outer):
                    copy.wait_send()
            for slot in range(4):
                for copy in keep(slot, c, shard_of(slot, me, outer)):
                    copy.wait()
            results(c, outer).wait_send()


def per_device_line(
    latent_codes, latent_scales, rope_keys, lengths, query_latent, query_rope, new_latent, new_rope
):
    groups = 4
    layers, requests, span, width = latent_codes.shape
    pairs, rows = layers * requests, span // groups
    rope, blocks = rope_keys.shape[-1], latent_scales.shape[-1]
    tokens, heads = query_latent.shape[2:4]
    half = tokens * heads
    codes = latent_codes.reshape(pairs, rows, groups, width).transpose(0, 2, 1, 3)
    ropes = rope_keys.reshape(pairs, rows, groups, rope).transpose(0, 2, 3, 1)
    scales = latent_scales.reshape(pairs, rows, groups, blocks).transpose(0, 2, 3, 1)
    aux = jnp.concatenate(
        [ropes, scales, jnp.zeros((pairs, groups, AUX - rope - blocks, rows), jnp.bfloat16)], axis=2
    )
    any_spec = pl.BlockSpec(memory_space=pl.ANY)
    vmem_spec = pl.BlockSpec(memory_space=pltpu.VMEM)
    dma = pltpu.SemaphoreType.DMA
    bf16, f32 = jnp.bfloat16, jnp.float32
    att, cache, caux = pl.pallas_call(
        _relay_kernel,
        out_shape=(
            jax.ShapeDtypeStruct((pairs, half, width), bf16),
            jax.ShapeDtypeStruct((pairs, groups, rows, width), bf16),
            jax.ShapeDtypeStruct((pairs, groups, AUX, rows), bf16),
        ),
        in_specs=[pl.BlockSpec(memory_space=pltpu.SMEM), any_spec, any_spec, any_spec, any_spec,
                  vmem_spec, vmem_spec],
        out_specs=(vmem_spec, any_spec, any_spec),
        scratch_shapes=[
            pltpu.VMEM((4, pairs, groups, rows, width), bf16),
            pltpu.VMEM((4, pairs, groups, AUX, rows), bf16),
            pltpu.VMEM((pairs, 2, half, width), bf16),
            pltpu.VMEM((pairs, 2, half, rope), bf16),
            pltpu.VMEM((pairs, 128, width), bf16),
            pltpu.VMEM((pairs, 128, rope), bf16),
            pltpu.VMEM((pairs, half, width), bf16),
            pltpu.VMEM((2 * half, width), f32),
            pltpu.VMEM((2 * half, 128), f32),
            pltpu.VMEM((2 * half, 128), f32),
            dma((4,)), dma((2, 4, pairs)), dma((2, 4, pairs)), dma((2, 4, pairs)),
            dma((2, pairs)), dma((2, pairs)), dma((2, 4, pairs)), dma((2, 4, pairs)),
            dma((pairs,)), dma((pairs,)),
        ],
        compiler_params=pltpu.CompilerParams(
            collective_id=0, has_side_effects=True, vmem_limit_bytes=40 << 20
        ),
    )(
        lengths, codes, aux,
        query_latent.reshape(pairs, half, width), query_rope.reshape(pairs, half, rope),
        new_latent.reshape(pairs, tokens, width), new_rope.reshape(pairs, tokens, rope),
    )
    spread = caux.reshape(layers, requests, groups, AUX, rows)

    def as_cache(values):
        return values.transpose(0, 1, 2, 4, 3).reshape(layers, requests, span, 1, values.shape[3])

    return (
        att.reshape(query_latent.shape),
        cache.reshape(layers, requests, span, 1, width),
        as_cache(spread[:, :, :, rope:rope + blocks]),
        as_cache(spread[:, :, :, :rope]),
    )


def solution(mesh):
    placed = (
        P(None, ("group", "req", "sub"), "seq", None),
        P(None, ("group", "req", "sub"), "seq", None),
        P(None, ("group", "req", "sub"), "seq", None),
        P(("group", "req", "sub")),
        P(None, ("group", "req", "sub"), None, "seq", None),
        P(None, ("group", "req", "sub"), None, "seq", None),
        P(None, ("group", "req", "sub"), None, None),
        P(None, ("group", "req", "sub"), None, None),
    )
    return jax.shard_map(
        per_device_line if mesh.shape["seq"] == 4 else per_device,
        mesh=mesh,
        in_specs=placed,
        out_specs=(
            P(None, ("group", "req", "sub"), None, "seq", None),
            P(None, ("group", "req", "sub"), None, "seq", None),
            P(None, ("group", "req", "sub"), None, "seq", None),
            P(None, ("group", "req", "sub"), None, "seq", None),
        ),
        check_vma=False,
    )
```

```python
import jax
import jax.numpy as jnp
from jax import lax
from jax.experimental import pallas as pl
from jax.experimental.pallas import tpu as pltpu
from jax.sharding import PartitionSpec as P

softmax_gain = 192.0 ** (-0.5)
masked_score = -1e30


def dequantize(code_values, scale_values):
    blocks = scale_values.shape[-1]
    latent_width = code_values.shape[-1]
    shaped = code_values.astype(jnp.float32).reshape(
        code_values.shape[:-1] + (blocks, latent_width // blocks)
    )
    scaled = shaped * scale_values.astype(jnp.float32)[..., None]
    return scaled.reshape(code_values.shape).astype(jnp.bfloat16)


def shard_partial(
    lat_query, rope_query, key_rows, rope_rows, usable, new_keys, new_rope_rows, holds_new
):
    tokens_new, head_count, latent_width = lat_query.shape
    query_rows = lat_query.reshape(tokens_new * head_count, latent_width)
    query_pos = rope_query.reshape(tokens_new * head_count, rope_query.shape[-1])
    scores = jnp.dot(query_rows, key_rows.T, preferred_element_type=jnp.float32)
    scores = (
        scores + jnp.dot(query_pos, rope_rows.T, preferred_element_type=jnp.float32)
    ) * softmax_gain
    fresh_scores = jnp.dot(query_rows, new_keys.T, preferred_element_type=jnp.float32)
    fresh_scores = (
        fresh_scores + jnp.dot(query_pos, new_rope_rows.T, preferred_element_type=jnp.float32)
    ) * softmax_gain
    token_of_row = jnp.arange(tokens_new * head_count, dtype=jnp.int32) // head_count
    causal = (jnp.arange(tokens_new, dtype=jnp.int32)[None, :] <= token_of_row[:, None]) & holds_new
    scores = jnp.where(usable[None, :], scores, masked_score)
    fresh_scores = jnp.where(causal, fresh_scores, masked_score)
    group_peak = jnp.maximum(jnp.max(scores, 1), jnp.max(fresh_scores, 1)).astype(jnp.bfloat16)
    peak_float = group_peak.astype(jnp.float32)[:, None]
    weights = jnp.where(usable[None, :], jnp.exp(scores - peak_float), 0.0).astype(jnp.bfloat16)
    fresh_weights = jnp.where(causal, jnp.exp(fresh_scores - peak_float), 0.0).astype(jnp.bfloat16)
    group_total = jnp.sum(weights.astype(jnp.float32), 1) + jnp.sum(
        fresh_weights.astype(jnp.float32), 1
    )
    group_sum = jnp.dot(weights, key_rows, preferred_element_type=jnp.float32)
    group_sum = group_sum + jnp.dot(fresh_weights, new_keys, preferred_element_type=jnp.float32)
    return (
        group_sum.astype(jnp.bfloat16).reshape(tokens_new, head_count, latent_width),
        group_peak.reshape(tokens_new, head_count),
        group_total.astype(jnp.bfloat16).reshape(tokens_new, head_count),
    )


def merge_groups(pieces):
    group_sum, group_peak, group_total = pieces
    peak_float = group_peak.astype(jnp.float32)
    overall = jnp.max(peak_float, 0)
    factor = jnp.exp(peak_float - overall)
    numerator = jnp.sum(factor[..., None] * group_sum.astype(jnp.float32), 0)
    denominator = jnp.sum(factor * group_total.astype(jnp.float32), 0)
    return (numerator / denominator[..., None]).astype(jnp.bfloat16)


def per_device(
    latent_codes, latent_scales, rope_keys, lengths, query_latent, query_rope, new_latent, new_rope
):
    shard_count = lax.axis_size("seq")
    seq_index = lax.axis_index("seq")
    layer_count, request_count, span, latent_width = latent_codes.shape
    lat_query, rope_query = (
        lax.all_gather(query_latent, "seq", axis=3, tiled=True),
        lax.all_gather(query_rope, "seq", axis=3, tiled=True),
    )

    def regroup_rows(values):
        return values.reshape(
            values.shape[0], values.shape[1], span // shard_count, shard_count, values.shape[-1]
        )

    codes_moved, scales_moved, rope_moved = (
        lax.all_to_all(regroup_rows(latent_codes), "seq", split_axis=3, concat_axis=2, tiled=True),
        lax.all_to_all(regroup_rows(latent_scales), "seq", split_axis=3, concat_axis=2, tiled=True),
        lax.all_to_all(regroup_rows(rope_keys), "seq", split_axis=3, concat_axis=2, tiled=True),
    )
    offsets = jnp.arange(span, dtype=jnp.int32)
    key_rows = dequantize(latent_codes, latent_scales)
    positions = seq_index * span + offsets
    usable = positions[None, :] < lengths[:, None]
    holds_new = seq_index == 0
    per_request = jax.vmap(shard_partial, in_axes=(0, 0, 0, 0, 0, 0, 0, None))
    per_layer = jax.vmap(per_request, in_axes=(0, 0, 0, 0, None, 0, 0, None))
    group_sum, group_peak, group_total = per_layer(
        lat_query, rope_query, key_rows, rope_keys, usable, new_latent, new_rope, holds_new
    )
    attended = merge_groups(
        (
            lax.all_to_all(group_sum[None], "seq", split_axis=4, concat_axis=0, tiled=True),
            lax.all_to_all(group_peak[None], "seq", split_axis=4, concat_axis=0, tiled=True),
            lax.all_to_all(group_total[None], "seq", split_axis=4, concat_axis=0, tiled=True),
        )
    )
    return (attended, codes_moved, scales_moved, rope_moved)


def _relay_kernel(
    len_ref, codes_ref, rope_ref, scale_ref, q_ref, qr_ref, new_ref, newr_ref,
    att_ref, cache_ref, crope_ref, cscale_ref,
    kbuf, abuf, raw, rawr, raws, stage, turned, qbuf, qrbuf, nkbuf, nrbuf, result, acc, peak, total,
    load_sem, out_sem, send_sem, recv_sem, q_send, q_recv, f_send, f_recv, r_send, r_recv,
):
    pairs, span, width = codes_ref.shape
    groups = 4
    rows = span // groups
    half = q_ref.shape[1]
    rope = qr_ref.shape[2]
    blocks = scale_ref.shape[1]
    heads = half // new_ref.shape[1]
    fresh = new_ref.shape[1]
    tail = groups * rope
    me = lax.axis_index("seq")
    inner = (me == 1) | (me == 2)
    outer = (me - 1) * 3
    across = 3 - me
    hub = 1 + me // 3
    side = me // 2

    def neighbour_signal(target):
        pl.semaphore_signal(
            pltpu.get_barrier_semaphore(), inc=1, device_id={"seq": target},
            device_id_type=pl.DeviceIdType.MESH,
        )

    def load(c):
        return (
            pltpu.make_async_copy(codes_ref.at[c], raw.at[c], load_sem.at[0, c]),
            pltpu.make_async_copy(rope_ref.at[c], rawr.at[c], load_sem.at[1, c]),
            pltpu.make_async_copy(scale_ref.at[c], raws.at[c], load_sem.at[2, c]),
            pltpu.make_async_copy(q_ref.at[c], qbuf.at[c, 0], load_sem.at[3, c]),
            pltpu.make_async_copy(qr_ref.at[c], qrbuf.at[c, 0], load_sem.at[4, c]),
        )

    def start(copies):
        for copy in copies:
            copy.start()

    for c in range(pairs):
        start(load(c))

    @pl.when(inner)
    def _():
        neighbour_signal(outer)
        neighbour_signal(across)

    @pl.when(jnp.logical_not(inner))
    def _():
        neighbour_signal(hub)

    def prepare(c):
        for copy in load(c):
            copy.wait()
        for b in range(width // 128):
            stage[b] = raw[c, :, b * 128:(b + 1) * 128].astype(jnp.float32)
        for k in range(groups):
            for b in range(width // 128):
                kbuf[0, c, k // 2, (k % 2) * rows:(k % 2 + 1) * rows, b * 128:(b + 1) * 128] = (
                    stage[b, pl.ds(k, rows, stride=groups), :].astype(jnp.bfloat16)
                )
        turned[...] = jnp.concatenate(
            [rawr[c].astype(jnp.float32), raws[c].astype(jnp.float32),
             jnp.zeros((128 - rope - blocks, span), jnp.float32)], axis=0
        ).T
        scales = []
        for k in range(groups):
            piece = turned[pl.ds(k, rows, stride=groups), :].T
            abuf[0, c, k * rope:(k + 1) * rope, :] = piece[0:rope].astype(jnp.bfloat16)
            scales.append(piece[rope:rope + blocks])
        abuf[0, c, tail:, :] = jnp.concatenate(scales, axis=0).astype(jnp.bfloat16)

    def remote(src, dst, send, recv, target):
        return pltpu.make_async_remote_copy(
            src_ref=src, dst_ref=dst, send_sem=send, recv_sem=recv,
            device_id={"seq": target}, device_id_type=pl.DeviceIdType.MESH,
        )

    def shard_head(src, dst, c, target, first):
        return (
            remote(abuf.at[src, c], abuf.at[dst, c],
                   send_sem.at[1, dst, c], recv_sem.at[1, dst, c], target),
            remote(kbuf.at[src, c, first], kbuf.at[dst, c, first],
                   send_sem.at[0, dst, c], recv_sem.at[0, dst, c], target),
        )

    def shard_rest(src, dst, c, target, first):
        return (
            remote(kbuf.at[src, c, 1 - first], kbuf.at[dst, c, 1 - first],
                   send_sem.at[2, dst, c], recv_sem.at[2, dst, c], target),
        )

    def shard(src, dst, c, target, first):
        return shard_head(src, dst, c, target, first) + shard_rest(src, dst, c, target, first)

    def queries(c, target):
        return (
            remote(qbuf.at[c, 0], qbuf.at[c, 1], q_send.at[0, c], q_recv.at[0, c], target),
            remote(qrbuf.at[c, 0], qrbuf.at[c, 1], q_send.at[1, c], q_recv.at[1, c], target),
        )

    def shard_of(slot, own, partner):
        base = own + (slot % 2) * (partner - own)
        return base + (slot // 2) * (3 - 2 * base)

    def key_part(slot, c, group):
        return kbuf.at[slot, c, group // 2, pl.ds(pl.multiple_of((group % 2) * rows, rows), rows)]

    def rope_part(slot, c, group):
        return abuf.at[slot, c, pl.ds(pl.multiple_of(group * rope, rope), rope)]

    def cache_part(c, place):
        return cache_ref.at[c, pl.ds(pl.multiple_of(place * rows, rows), rows)]

    def crope_part(c, place):
        return crope_ref.at[c, :, pl.ds(pl.multiple_of(place * rows, rows), rows)]

    def handover(slot, c, group, place, target):
        kept = slot + 1 - jnp.minimum(slot, 1)
        return (
            remote(key_part(slot, c, group), cache_part(c, place),
                   f_send.at[0, slot, c], f_recv.at[0, slot, c], target),
            remote(rope_part(slot, c, group), crope_part(c, place),
                   f_send.at[1, slot, c], f_recv.at[1, slot, c], target),
            remote(abuf.at[slot, c, pl.ds(tail, 16)], abuf.at[kept, c, pl.ds(tail, 16)],
                   f_send.at[2, slot, c], f_recv.at[2, slot, c], target),
        )

    def keep(slot, c, place):
        return (
            pltpu.make_async_copy(key_part(slot, c, me), cache_part(c, place), out_sem.at[0, slot, c]),
            pltpu.make_async_copy(rope_part(slot, c, me), crope_part(c, place), out_sem.at[1, slot, c]),
        )

    def keep_scales(slot, c, place):
        tile = abuf[slot, c, tail:tail + 16, :].astype(jnp.float32)
        mine = tile[0:blocks]
        for k in range(1, groups):
            mine = jnp.where(me == k, tile[k * blocks:(k + 1) * blocks], mine)
        cscale_ref[c, :, pl.ds(pl.multiple_of(place * rows, rows), rows)] = mine.astype(jnp.bfloat16)

    def results(c, target):
        return remote(result.at[c], att_ref.at[c], r_send.at[c], r_recv.at[c], target)

    prepare(0)

    @pl.when(jnp.logical_not(inner))
    def _():
        pl.semaphore_wait(pltpu.get_barrier_semaphore(), 1)

        @pl.loop(0, pairs)
        def _(c):
            copies = shard(0, 1, c, hub, side) + queries(c, hub)
            start(copies)
            start(keep(0, c, me))
            keep_scales(0, c, me)

            @pl.when(c + 1 < pairs)
            def _():
                prepare(c + 1)

            for copy in copies:
                copy.wait_send()

        @pl.loop(0, pairs)
        def _(c):
            for slot in (0, 2, 3):
                place = shard_of(slot, hub, me)
                for copy in handover(slot, c, me, place, hub):
                    copy.wait_recv()
                keep_scales(max(slot, 1), c, place)
            results(c, hub).wait_recv()
            for copy in keep(0, c, me):
                copy.wait()

    @pl.when(inner)
    def _():
        pl.semaphore_wait(pltpu.get_barrier_semaphore(), 2)

        @pl.loop(0, pairs)
        def _(c):
            @pl.when(c < 2)
            def _():
                start(shard(0, 2, c, across, 1 - side))

            start(handover(0, c, outer, me, outer))
            start(keep(0, c, me))
            keep_scales(0, c, me)
            nkbuf[c] = jnp.zeros(nkbuf.shape[1:], nkbuf.dtype)
            nrbuf[c] = jnp.zeros(nrbuf.shape[1:], nrbuf.dtype)
            nkbuf[c, 0:fresh, :] = new_ref[c]
            nrbuf[c, 0:fresh, :] = newr_ref[c]

            @pl.when(c + 1 < pairs)
            def _():
                prepare(c + 1)

        def relay(c):
            for copy in shard(0, 1, c, outer, side):
                copy.wait_recv()
            start(shard(1, 3, c, across, 1 - side))
            start(keep(1, c, outer))

        relay(0)
        start(shard(0, 2, 2, across, 1 - side))

        @pl.loop(0, pairs)
        def _(c):
            @pl.when(c + 1 < pairs)
            def _():
                relay(c + 1)

            @pl.when(c + 3 < pairs)
            def _():
                start(shard(0, 2, c + 3, across, 1 - side))

            for copy in queries(c, outer):
                copy.wait_recv()
            q = qbuf[c].reshape(2 * half, width)
            qr = qrbuf[c].reshape(2 * half, rope)
            dims = (((1,), (1,)), ((), ()))
            s = lax.dot_general(q, nkbuf[c], dims, preferred_element_type=jnp.float32)
            s = s + lax.dot_general(qr, nrbuf[c], dims, preferred_element_type=jnp.float32)
            s = s * softmax_gain
            token = (lax.broadcasted_iota(jnp.int32, s.shape, 0) % half) // heads
            s = jnp.where(lax.broadcasted_iota(jnp.int32, s.shape, 1) <= token, s, masked_score)
            m = jnp.max(s, axis=1, keepdims=True)
            w = jnp.exp(s - m).astype(jnp.bfloat16)
            peak[...] = jnp.broadcast_to(m, peak.shape)
            total[...] = jnp.broadcast_to(
                jnp.sum(w.astype(jnp.float32), axis=1, keepdims=True), total.shape
            )
            acc[...] = jnp.dot(w, nkbuf[c], preferred_element_type=jnp.float32)
            length = len_ref[c % len_ref.shape[0]]

            @pl.loop(0, 8)
            def _(step):
                slot = step // 2
                part = side + (step % 2) * (1 - 2 * side)
                place = shard_of(slot, me, outer)

                @pl.when((slot >= 2) & (step % 2 == 0))
                def _():
                    for copy in shard_head(0, slot, c, across, side):
                        copy.wait_recv()
                    start(handover(slot, c, outer, place, outer))
                    start(keep(slot, c, place))

                @pl.when((slot >= 2) & (step % 2 == 1))
                def _():
                    for copy in shard_rest(0, slot, c, across, side):
                        copy.wait_recv()

                @pl.when((slot >= 1) & (step % 2 == 0))
                def _():
                    keep_scales(slot, c, place)

                scales = abuf[slot, c, tail:tail + 16, :].astype(jnp.float32)
                scales = jnp.where(side + step % 2 == 1, scales[8:16], scales[0:8]).T
                keys = []
                for k in range(2):
                    codes = kbuf[slot, c, part, k * rows:(k + 1) * rows, :].astype(jnp.float32)
                    keys.append(jnp.concatenate([
                        codes[:, b * 128:(b + 1) * 128] * scales[:, k * blocks + b:k * blocks + b + 1]
                        for b in range(blocks)
                    ], axis=1).astype(jnp.bfloat16))
                keys = jnp.concatenate(keys, axis=0)
                base = pl.multiple_of(part * 2 * rope, 2 * rope)
                ropes = jnp.concatenate(
                    [abuf[slot, c, pl.ds(base, rope), :], abuf[slot, c, pl.ds(base + rope, rope), :]],
                    axis=1,
                )
                q = qbuf[c].reshape(2 * half, width)
                qr = qrbuf[c].reshape(2 * half, rope)
                s = lax.dot_general(q, keys, dims, preferred_element_type=jnp.float32)
                s = s + jnp.dot(qr, ropes, preferred_element_type=jnp.float32)
                s = s * softmax_gain
                column = lax.broadcasted_iota(jnp.int32, (1, 2 * rows), 1)
                position = place * span + (column % rows) * groups + 2 * part + column // rows
                s = jnp.where(position < length, s, masked_score)
                before = peak[:, 0:1]
                m = jnp.maximum(before, jnp.max(s, axis=1, keepdims=True))
                factor = jnp.exp(before - m)
                w = jnp.exp(s - m).astype(jnp.bfloat16)
                peak[...] = jnp.broadcast_to(m, peak.shape)
                total[...] = factor * total[...] + jnp.sum(w.astype(jnp.float32), axis=1, keepdims=True)
                acc[...] = factor * acc[...] + jnp.dot(w, keys, preferred_element_type=jnp.float32)

            result[c] = (acc[half:, :] / total[half:, 0:1]).astype(jnp.bfloat16)
            results(c, outer).start()
            att_ref[c] = (acc[:half, :] / total[:half, 0:1]).astype(jnp.bfloat16)

        @pl.loop(0, pairs)
        def _(c):
            for copy in shard(0, 2, c, across, 1 - side) + shard(1, 3, c, across, 1 - side):
                copy.wait_send()
            for slot in (0, 2, 3):
                for copy in handover(slot, c, outer, shard_of(slot, me, outer), outer):
                    copy.wait_send()
            for slot in range(4):
                for copy in keep(slot, c, shard_of(slot, me, outer)):
                    copy.wait()
            results(c, outer).wait_send()


def per_device_line(
    latent_codes, latent_scales, rope_keys, lengths, query_latent, query_rope, new_latent, new_rope
):
    layers, requests, span, width = latent_codes.shape
    pairs, rows = layers * requests, span // 4
    rope, blocks = rope_keys.shape[-1], latent_scales.shape[-1]
    tokens, heads = query_latent.shape[2:4]
    half = tokens * heads
    aux = 4 * rope + 16
    hbm_spec = pl.BlockSpec(memory_space=pltpu.HBM)
    any_spec = pl.BlockSpec(memory_space=pl.ANY)
    vmem_spec = pl.BlockSpec(memory_space=pltpu.VMEM)
    dma = pltpu.SemaphoreType.DMA
    bf16, f32 = jnp.bfloat16, jnp.float32
    att, cache, crope, cscale = pl.pallas_call(
        _relay_kernel,
        out_shape=(
            jax.ShapeDtypeStruct((pairs, half, width), bf16),
            jax.ShapeDtypeStruct((pairs, span, width), bf16),
            jax.ShapeDtypeStruct((pairs, rope, span), bf16),
            jax.ShapeDtypeStruct((pairs, blocks, span), bf16),
        ),
        in_specs=[pl.BlockSpec(memory_space=pltpu.SMEM)] + [hbm_spec] * 5 + [vmem_spec] * 2,
        out_specs=(vmem_spec, any_spec, any_spec, vmem_spec),
        scratch_shapes=[
            pltpu.VMEM((4, pairs, 2, 2 * rows, width), bf16),
            pltpu.VMEM((4, pairs, aux, rows), bf16),
            pltpu.VMEM((pairs, span, width), bf16),
            pltpu.VMEM((pairs, rope, span), bf16),
            pltpu.VMEM((pairs, blocks, span), bf16),
            pltpu.VMEM((width // 128, span, 128), f32),
            pltpu.VMEM((span, 128), f32),
            pltpu.VMEM((pairs, 2, half, width), bf16),
            pltpu.VMEM((pairs, 2, half, rope), bf16),
            pltpu.VMEM((pairs, 128, width), bf16),
            pltpu.VMEM((pairs, 128, rope), bf16),
            pltpu.VMEM((pairs, half, width), bf16),
            pltpu.VMEM((2 * half, width), f32),
            pltpu.VMEM((2 * half, 128), f32),
            pltpu.VMEM((2 * half, 128), f32),
            dma((5, pairs)), dma((2, 4, pairs)), dma((3, 4, pairs)), dma((3, 4, pairs)),
            dma((2, pairs)), dma((2, pairs)), dma((3, 4, pairs)), dma((3, 4, pairs)),
            dma((pairs,)), dma((pairs,)),
        ],
        compiler_params=pltpu.CompilerParams(
            collective_id=0, has_side_effects=True, vmem_limit_bytes=40 << 20
        ),
    )(
        lengths, latent_codes.reshape(pairs, span, width),
        rope_keys.transpose(0, 1, 3, 2).reshape(pairs, rope, span),
        latent_scales.transpose(0, 1, 3, 2).reshape(pairs, blocks, span),
        query_latent.reshape(pairs, half, width), query_rope.reshape(pairs, half, rope),
        new_latent.reshape(pairs, tokens, width), new_rope.reshape(pairs, tokens, rope),
    )

    def as_cache(values):
        flipped = values.reshape(layers, requests, values.shape[1], span).transpose(0, 1, 3, 2)
        return flipped.reshape(layers, requests, span, 1, values.shape[1])

    return (
        att.reshape(query_latent.shape),
        cache.reshape(layers, requests, span, 1, width),
        as_cache(cscale),
        as_cache(crope),
    )


def solution(mesh):
    placed = (
        P(None, ("group", "req", "sub"), "seq", None),
        P(None, ("group", "req", "sub"), "seq", None),
        P(None, ("group", "req", "sub"), "seq", None),
        P(("group", "req", "sub")),
        P(None, ("group", "req", "sub"), None, "seq", None),
        P(None, ("group", "req", "sub"), None, "seq", None),
        P(None, ("group", "req", "sub"), None, None),
        P(None, ("group", "req", "sub"), None, None),
    )
    return jax.shard_map(
        per_device_line if mesh.shape["seq"] == 4 else per_device,
        mesh=mesh,
        in_specs=placed,
        out_specs=(
            P(None, ("group", "req", "sub"), None, "seq", None),
            P(None, ("group", "req", "sub"), None, "seq", None),
            P(None, ("group", "req", "sub"), None, "seq", None),
            P(None, ("group", "req", "sub"), None, "seq", None),
        ),
        check_vma=False,
    )
```

```python
import jax
import jax.numpy as jnp
from jax import lax
from jax.experimental import pallas as pl
from jax.experimental.pallas import tpu as pltpu
from jax.sharding import PartitionSpec as P

softmax_gain = 192.0 ** (-0.5)
masked_score = -1e30


def dequantize(code_values, scale_values):
    blocks = scale_values.shape[-1]
    latent_width = code_values.shape[-1]
    shaped = code_values.astype(jnp.float32).reshape(
        code_values.shape[:-1] + (blocks, latent_width // blocks)
    )
    scaled = shaped * scale_values.astype(jnp.float32)[..., None]
    return scaled.reshape(code_values.shape).astype(jnp.bfloat16)


def shard_partial(
    lat_query, rope_query, key_rows, rope_rows, usable, new_keys, new_rope_rows, holds_new
):
    tokens_new, head_count, latent_width = lat_query.shape
    query_rows = lat_query.reshape(tokens_new * head_count, latent_width)
    query_pos = rope_query.reshape(tokens_new * head_count, rope_query.shape[-1])
    scores = jnp.dot(query_rows, key_rows.T, preferred_element_type=jnp.float32)
    scores = (
        scores + jnp.dot(query_pos, rope_rows.T, preferred_element_type=jnp.float32)
    ) * softmax_gain
    fresh_scores = jnp.dot(query_rows, new_keys.T, preferred_element_type=jnp.float32)
    fresh_scores = (
        fresh_scores + jnp.dot(query_pos, new_rope_rows.T, preferred_element_type=jnp.float32)
    ) * softmax_gain
    token_of_row = jnp.arange(tokens_new * head_count, dtype=jnp.int32) // head_count
    causal = (jnp.arange(tokens_new, dtype=jnp.int32)[None, :] <= token_of_row[:, None]) & holds_new
    scores = jnp.where(usable[None, :], scores, masked_score)
    fresh_scores = jnp.where(causal, fresh_scores, masked_score)
    group_peak = jnp.maximum(jnp.max(scores, 1), jnp.max(fresh_scores, 1)).astype(jnp.bfloat16)
    peak_float = group_peak.astype(jnp.float32)[:, None]
    weights = jnp.where(usable[None, :], jnp.exp(scores - peak_float), 0.0).astype(jnp.bfloat16)
    fresh_weights = jnp.where(causal, jnp.exp(fresh_scores - peak_float), 0.0).astype(jnp.bfloat16)
    group_total = jnp.sum(weights.astype(jnp.float32), 1) + jnp.sum(
        fresh_weights.astype(jnp.float32), 1
    )
    group_sum = jnp.dot(weights, key_rows, preferred_element_type=jnp.float32)
    group_sum = group_sum + jnp.dot(fresh_weights, new_keys, preferred_element_type=jnp.float32)
    return (
        group_sum.astype(jnp.bfloat16).reshape(tokens_new, head_count, latent_width),
        group_peak.reshape(tokens_new, head_count),
        group_total.astype(jnp.bfloat16).reshape(tokens_new, head_count),
    )


def merge_groups(pieces):
    group_sum, group_peak, group_total = pieces
    peak_float = group_peak.astype(jnp.float32)
    overall = jnp.max(peak_float, 0)
    factor = jnp.exp(peak_float - overall)
    numerator = jnp.sum(factor[..., None] * group_sum.astype(jnp.float32), 0)
    denominator = jnp.sum(factor * group_total.astype(jnp.float32), 0)
    return (numerator / denominator[..., None]).astype(jnp.bfloat16)


def per_device(
    latent_codes, latent_scales, rope_keys, lengths, query_latent, query_rope, new_latent, new_rope
):
    shard_count = lax.axis_size("seq")
    seq_index = lax.axis_index("seq")
    layer_count, request_count, span, latent_width = latent_codes.shape
    lat_query, rope_query = (
        lax.all_gather(query_latent, "seq", axis=3, tiled=True),
        lax.all_gather(query_rope, "seq", axis=3, tiled=True),
    )

    def regroup_rows(values):
        return values.reshape(
            values.shape[0], values.shape[1], span // shard_count, shard_count, values.shape[-1]
        )

    codes_moved, scales_moved, rope_moved = (
        lax.all_to_all(regroup_rows(latent_codes), "seq", split_axis=3, concat_axis=2, tiled=True),
        lax.all_to_all(regroup_rows(latent_scales), "seq", split_axis=3, concat_axis=2, tiled=True),
        lax.all_to_all(regroup_rows(rope_keys), "seq", split_axis=3, concat_axis=2, tiled=True),
    )
    offsets = jnp.arange(span, dtype=jnp.int32)
    key_rows = dequantize(latent_codes, latent_scales)
    positions = seq_index * span + offsets
    usable = positions[None, :] < lengths[:, None]
    holds_new = seq_index == 0
    per_request = jax.vmap(shard_partial, in_axes=(0, 0, 0, 0, 0, 0, 0, None))
    per_layer = jax.vmap(per_request, in_axes=(0, 0, 0, 0, None, 0, 0, None))
    group_sum, group_peak, group_total = per_layer(
        lat_query, rope_query, key_rows, rope_keys, usable, new_latent, new_rope, holds_new
    )
    attended = merge_groups(
        (
            lax.all_to_all(group_sum[None], "seq", split_axis=4, concat_axis=0, tiled=True),
            lax.all_to_all(group_peak[None], "seq", split_axis=4, concat_axis=0, tiled=True),
            lax.all_to_all(group_total[None], "seq", split_axis=4, concat_axis=0, tiled=True),
        )
    )
    return (attended, codes_moved, scales_moved, rope_moved)


def _relay_kernel(
    len_ref, codes_ref, rope_ref, scale_ref, q_ref, qr_ref, new_ref, newr_ref,
    att_ref, cache_ref, crope_ref, cscale_ref,
    kbuf, abuf, raw, rawr, raws, stage, turned, qbuf, qrbuf, nkbuf, nrbuf, result, acc, peak, total,
    load_sem, out_sem, send_sem, recv_sem, q_send, q_recv, f_send, f_recv, r_send, r_recv,
):
    pairs, span, width = codes_ref.shape
    groups = 4
    rows = span // groups
    half = q_ref.shape[1]
    rope = qr_ref.shape[2]
    blocks = scale_ref.shape[1]
    heads = half // new_ref.shape[1]
    fresh = new_ref.shape[1]
    tail = groups * rope
    me = lax.axis_index("seq")
    inner = (me == 1) | (me == 2)
    outer = (me - 1) * 3
    across = 3 - me
    hub = 1 + me // 3
    side = me // 2

    def neighbour_signal(target):
        pl.semaphore_signal(
            pltpu.get_barrier_semaphore(), inc=1, device_id={"seq": target},
            device_id_type=pl.DeviceIdType.MESH,
        )

    def load(c):
        return (
            pltpu.make_async_copy(codes_ref.at[c], raw.at[c], load_sem.at[0, c]),
            pltpu.make_async_copy(rope_ref.at[c], rawr.at[c], load_sem.at[1, c]),
            pltpu.make_async_copy(scale_ref.at[c], raws.at[c], load_sem.at[2, c]),
            pltpu.make_async_copy(q_ref.at[c], qbuf.at[c, 0], load_sem.at[3, c]),
            pltpu.make_async_copy(qr_ref.at[c], qrbuf.at[c, 0], load_sem.at[4, c]),
        )

    def start(copies):
        for copy in copies:
            copy.start()

    for c in range(pairs):
        start(load(c))

    @pl.when(inner)
    def _():
        neighbour_signal(outer)
        neighbour_signal(across)

    @pl.when(jnp.logical_not(inner))
    def _():
        neighbour_signal(hub)

    def prepare(c):
        for copy in load(c):
            copy.wait()
        for b in range(width // 128):
            stage[b] = raw[c, :, b * 128:(b + 1) * 128].astype(jnp.float32)
        for k in range(groups):
            for b in range(width // 128):
                kbuf[0, c, k // 2, (k % 2) * rows:(k % 2 + 1) * rows, b * 128:(b + 1) * 128] = (
                    stage[b, pl.ds(k, rows, stride=groups), :].astype(jnp.bfloat16)
                )
        turned[...] = jnp.concatenate(
            [rawr[c].astype(jnp.float32), raws[c].astype(jnp.float32),
             jnp.zeros((128 - rope - blocks, span), jnp.float32)], axis=0
        ).T
        scales = []
        for k in range(groups):
            piece = turned[pl.ds(k, rows, stride=groups), :].T
            abuf[0, c, k * rope:(k + 1) * rope, :] = piece[0:rope].astype(jnp.bfloat16)
            scales.append(piece[rope:rope + blocks])
        abuf[0, c, tail:, :] = jnp.concatenate(scales, axis=0).astype(jnp.bfloat16)

    def remote(src, dst, send, recv, target):
        return pltpu.make_async_remote_copy(
            src_ref=src, dst_ref=dst, send_sem=send, recv_sem=recv,
            device_id={"seq": target}, device_id_type=pl.DeviceIdType.MESH,
        )

    def shard_head(src, dst, c, target, first):
        return (
            remote(abuf.at[src, c], abuf.at[dst, c],
                   send_sem.at[1, dst, c], recv_sem.at[1, dst, c], target),
            remote(kbuf.at[src, c, first], kbuf.at[dst, c, first],
                   send_sem.at[0, dst, c], recv_sem.at[0, dst, c], target),
        )

    def shard_rest(src, dst, c, target, first):
        return (
            remote(kbuf.at[src, c, 1 - first], kbuf.at[dst, c, 1 - first],
                   send_sem.at[2, dst, c], recv_sem.at[2, dst, c], target),
        )

    def shard(src, dst, c, target, first):
        return shard_head(src, dst, c, target, first) + shard_rest(src, dst, c, target, first)

    def queries(c, target):
        return (
            remote(qbuf.at[c, 0], qbuf.at[c, 1], q_send.at[0, c], q_recv.at[0, c], target),
            remote(qrbuf.at[c, 0], qrbuf.at[c, 1], q_send.at[1, c], q_recv.at[1, c], target),
        )

    def shard_of(slot, own, partner):
        base = own + (slot % 2) * (partner - own)
        return base + (slot // 2) * (3 - 2 * base)

    def key_part(slot, c, group):
        return kbuf.at[slot, c, group // 2, pl.ds(pl.multiple_of((group % 2) * rows, rows), rows)]

    def rope_part(slot, c, group):
        return abuf.at[slot, c, pl.ds(pl.multiple_of(group * rope, rope), rope)]

    def cache_part(c, place):
        return cache_ref.at[c, pl.ds(pl.multiple_of(place * rows, rows), rows)]

    def crope_part(c, place):
        return crope_ref.at[c, :, pl.ds(pl.multiple_of(place * rows, rows), rows)]

    def handover(slot, c, group, place, target):
        kept = slot + 1 - jnp.minimum(slot, 1)
        return (
            remote(key_part(slot, c, group), cache_part(c, place),
                   f_send.at[0, slot, c], f_recv.at[0, slot, c], target),
            remote(rope_part(slot, c, group), crope_part(c, place),
                   f_send.at[1, slot, c], f_recv.at[1, slot, c], target),
            remote(abuf.at[slot, c, pl.ds(tail, 16)], abuf.at[kept, c, pl.ds(tail, 16)],
                   f_send.at[2, slot, c], f_recv.at[2, slot, c], target),
        )

    def keep(slot, c, place):
        return (
            pltpu.make_async_copy(key_part(slot, c, me), cache_part(c, place), out_sem.at[0, slot, c]),
            pltpu.make_async_copy(rope_part(slot, c, me), crope_part(c, place), out_sem.at[1, slot, c]),
        )

    def keep_scales(slot, c, place):
        tile = abuf[slot, c, tail:tail + 16, :].astype(jnp.float32)
        mine = tile[0:blocks]
        for k in range(1, groups):
            mine = jnp.where(me == k, tile[k * blocks:(k + 1) * blocks], mine)
        cscale_ref[c, :, pl.ds(pl.multiple_of(place * rows, rows), rows)] = mine.astype(jnp.bfloat16)

    def results(c, target):
        return remote(result.at[c], att_ref.at[c], r_send.at[c], r_recv.at[c], target)

    prepare(0)

    @pl.when(jnp.logical_not(inner))
    def _():
        pl.semaphore_wait(pltpu.get_barrier_semaphore(), 1)

        @pl.loop(0, pairs)
        def _(c):
            copies = shard(0, 1, c, hub, side) + queries(c, hub)
            start(copies)
            start(keep(0, c, me))
            keep_scales(0, c, me)

            @pl.when(c + 1 < pairs)
            def _():
                prepare(c + 1)

            for copy in copies:
                copy.wait_send()

        @pl.loop(0, pairs)
        def _(c):
            for slot in (0, 2, 3):
                place = shard_of(slot, hub, me)
                for copy in handover(slot, c, me, place, hub):
                    copy.wait_recv()
                keep_scales(max(slot, 1), c, place)
            results(c, hub).wait_recv()
            for copy in keep(0, c, me):
                copy.wait()

    @pl.when(inner)
    def _():
        pl.semaphore_wait(pltpu.get_barrier_semaphore(), 2)

        @pl.loop(0, pairs)
        def _(c):
            @pl.when(c < 2)
            def _():
                start(shard(0, 2, c, across, 1 - side))

            start(handover(0, c, outer, me, outer))
            start(keep(0, c, me))
            keep_scales(0, c, me)
            nkbuf[c] = jnp.zeros(nkbuf.shape[1:], nkbuf.dtype)
            nrbuf[c] = jnp.zeros(nrbuf.shape[1:], nrbuf.dtype)
            nkbuf[c, 0:fresh, :] = new_ref[c]
            nrbuf[c, 0:fresh, :] = newr_ref[c]

            @pl.when(c + 1 < pairs)
            def _():
                prepare(c + 1)

        def relay(c):
            for copy in shard(0, 1, c, outer, side):
                copy.wait_recv()
            start(shard(1, 3, c, across, 1 - side))
            start(keep(1, c, outer))

        relay(0)
        start(shard(0, 2, 2, across, 1 - side))

        @pl.loop(0, pairs)
        def _(c):
            @pl.when(c + 1 < pairs)
            def _():
                relay(c + 1)

            @pl.when(c + 3 < pairs)
            def _():
                start(shard(0, 2, c + 3, across, 1 - side))

            for copy in queries(c, outer):
                copy.wait_recv()
            q = qbuf[c].reshape(2 * half, width)
            qr = qrbuf[c].reshape(2 * half, rope)
            dims = (((1,), (1,)), ((), ()))
            s = lax.dot_general(q, nkbuf[c], dims, preferred_element_type=jnp.float32)
            s = s + lax.dot_general(qr, nrbuf[c], dims, preferred_element_type=jnp.float32)
            s = s * softmax_gain
            token = (lax.broadcasted_iota(jnp.int32, s.shape, 0) % half) // heads
            s = jnp.where(lax.broadcasted_iota(jnp.int32, s.shape, 1) <= token, s, masked_score)
            m = jnp.max(s, axis=1, keepdims=True)
            w = jnp.exp(s - m).astype(jnp.bfloat16)
            peak[...] = jnp.broadcast_to(m, peak.shape)
            total[...] = jnp.broadcast_to(
                jnp.sum(w.astype(jnp.float32), axis=1, keepdims=True), total.shape
            )
            acc[...] = jnp.dot(w, nkbuf[c], preferred_element_type=jnp.float32)
            length = len_ref[c % len_ref.shape[0]]

            @pl.loop(0, 8)
            def _(step):
                slot = step // 2
                part = side + (step % 2) * (1 - 2 * side)
                place = shard_of(slot, me, outer)

                @pl.when((slot >= 2) & (step % 2 == 0))
                def _():
                    for copy in shard_head(0, slot, c, across, side):
                        copy.wait_recv()
                    start(handover(slot, c, outer, place, outer))
                    start(keep(slot, c, place))

                @pl.when((slot >= 2) & (step % 2 == 1))
                def _():
                    for copy in shard_rest(0, slot, c, across, side):
                        copy.wait_recv()

                @pl.when((slot >= 1) & (step % 2 == 0))
                def _():
                    keep_scales(slot, c, place)

                scales = abuf[slot, c, tail:tail + 16, :].astype(jnp.float32)
                scales = jnp.where(side + step % 2 == 1, scales[8:16], scales[0:8]).T
                keys = []
                for k in range(2):
                    codes = kbuf[slot, c, part, k * rows:(k + 1) * rows, :].astype(jnp.float32)
                    keys.append(jnp.concatenate([
                        codes[:, b * 128:(b + 1) * 128] * scales[:, k * blocks + b:k * blocks + b + 1]
                        for b in range(blocks)
                    ], axis=1).astype(jnp.bfloat16))
                keys = jnp.concatenate(keys, axis=0)
                base = pl.multiple_of(part * 2 * rope, 2 * rope)
                ropes = jnp.concatenate(
                    [abuf[slot, c, pl.ds(base, rope), :], abuf[slot, c, pl.ds(base + rope, rope), :]],
                    axis=1,
                )
                q = qbuf[c].reshape(2 * half, width)
                qr = qrbuf[c].reshape(2 * half, rope)
                s = lax.dot_general(q, keys, dims, preferred_element_type=jnp.float32)
                s = s + jnp.dot(qr, ropes, preferred_element_type=jnp.float32)
                s = s * softmax_gain
                column = lax.broadcasted_iota(jnp.int32, (1, 2 * rows), 1)
                position = place * span + (column % rows) * groups + 2 * part + column // rows
                s = jnp.where(position < length, s, masked_score)
                before = peak[:, 0:1]
                m = jnp.maximum(before, jnp.max(s, axis=1, keepdims=True))
                factor = jnp.exp(before - m)
                w = jnp.exp(s - m).astype(jnp.bfloat16)
                peak[...] = jnp.broadcast_to(m, peak.shape)
                total[...] = factor * total[...] + jnp.sum(w.astype(jnp.float32), axis=1, keepdims=True)
                acc[...] = factor * acc[...] + jnp.dot(w, keys, preferred_element_type=jnp.float32)

            result[c] = (acc[half:, :] / total[half:, 0:1]).astype(jnp.bfloat16)
            results(c, outer).start()
            att_ref[c] = (acc[:half, :] / total[:half, 0:1]).astype(jnp.bfloat16)

        @pl.loop(0, pairs)
        def _(c):
            for copy in shard(0, 2, c, across, 1 - side) + shard(1, 3, c, across, 1 - side):
                copy.wait_send()
            for slot in (0, 2, 3):
                for copy in handover(slot, c, outer, shard_of(slot, me, outer), outer):
                    copy.wait_send()
            for slot in range(4):
                for copy in keep(slot, c, shard_of(slot, me, outer)):
                    copy.wait()
            results(c, outer).wait_send()


def per_device_line(
    latent_codes, latent_scales, rope_keys, lengths, query_latent, query_rope, new_latent, new_rope
):
    layers, requests, span, width = latent_codes.shape
    pairs, rows = layers * requests, span // 4
    rope, blocks = rope_keys.shape[-1], latent_scales.shape[-1]
    tokens, heads = query_latent.shape[2:4]
    half = tokens * heads
    aux = 4 * rope + 16
    hbm_spec = pl.BlockSpec(memory_space=pltpu.HBM)
    any_spec = pl.BlockSpec(memory_space=pl.ANY)
    vmem_spec = pl.BlockSpec(memory_space=pltpu.VMEM)
    dma = pltpu.SemaphoreType.DMA
    bf16, f32 = jnp.bfloat16, jnp.float32
    att, cache, crope, cscale = pl.pallas_call(
        _relay_kernel,
        out_shape=(
            jax.ShapeDtypeStruct((pairs, half, width), bf16),
            jax.ShapeDtypeStruct((pairs, span, width), bf16),
            jax.ShapeDtypeStruct((pairs, rope, span), bf16),
            jax.ShapeDtypeStruct((pairs, blocks, span), bf16),
        ),
        in_specs=[pl.BlockSpec(memory_space=pltpu.SMEM)] + [hbm_spec] * 5 + [vmem_spec] * 2,
        out_specs=(vmem_spec, any_spec, any_spec, vmem_spec),
        scratch_shapes=[
            pltpu.VMEM((4, pairs, 2, 2 * rows, width), bf16),
            pltpu.VMEM((4, pairs, aux, rows), bf16),
            pltpu.VMEM((pairs, span, width), bf16),
            pltpu.VMEM((pairs, rope, span), bf16),
            pltpu.VMEM((pairs, blocks, span), bf16),
            pltpu.VMEM((width // 128, span, 128), f32),
            pltpu.VMEM((span, 128), f32),
            pltpu.VMEM((pairs, 2, half, width), bf16),
            pltpu.VMEM((pairs, 2, half, rope), bf16),
            pltpu.VMEM((pairs, 128, width), bf16),
            pltpu.VMEM((pairs, 128, rope), bf16),
            pltpu.VMEM((pairs, half, width), bf16),
            pltpu.VMEM((2 * half, width), f32),
            pltpu.VMEM((2 * half, 128), f32),
            pltpu.VMEM((2 * half, 128), f32),
            dma((5, pairs)), dma((2, 4, pairs)), dma((3, 4, pairs)), dma((3, 4, pairs)),
            dma((2, pairs)), dma((2, pairs)), dma((3, 4, pairs)), dma((3, 4, pairs)),
            dma((pairs,)), dma((pairs,)),
        ],
        compiler_params=pltpu.CompilerParams(
            collective_id=0, has_side_effects=True, vmem_limit_bytes=60 << 20
        ),
    )(
        lengths, latent_codes.reshape(pairs, span, width),
        rope_keys.transpose(0, 1, 3, 2).reshape(pairs, rope, span),
        latent_scales.transpose(0, 1, 3, 2).reshape(pairs, blocks, span),
        query_latent.reshape(pairs, half, width), query_rope.reshape(pairs, half, rope),
        new_latent.reshape(pairs, tokens, width), new_rope.reshape(pairs, tokens, rope),
    )

    def as_cache(values):
        flipped = values.reshape(layers, requests, values.shape[1], span).transpose(0, 1, 3, 2)
        return flipped.reshape(layers, requests, span, 1, values.shape[1])

    return (
        att.reshape(query_latent.shape),
        cache.reshape(layers, requests, span, 1, width),
        as_cache(cscale),
        as_cache(crope),
    )


def solution(mesh):
    placed = (
        P(None, ("group", "req", "sub"), "seq", None),
        P(None, ("group", "req", "sub"), "seq", None),
        P(None, ("group", "req", "sub"), "seq", None),
        P(("group", "req", "sub")),
        P(None, ("group", "req", "sub"), None, "seq", None),
        P(None, ("group", "req", "sub"), None, "seq", None),
        P(None, ("group", "req", "sub"), None, None),
        P(None, ("group", "req", "sub"), None, None),
    )
    return jax.shard_map(
        per_device_line if mesh.shape["seq"] == 4 else per_device,
        mesh=mesh,
        in_specs=placed,
        out_specs=(
            P(None, ("group", "req", "sub"), None, "seq", None),
            P(None, ("group", "req", "sub"), None, "seq", None),
            P(None, ("group", "req", "sub"), None, "seq", None),
            P(None, ("group", "req", "sub"), None, "seq", None),
        ),
        check_vma=False,
    )
```

```python
import jax
import jax.numpy as jnp
from jax import lax
from jax.experimental import pallas as pl
from jax.experimental.pallas import tpu as pltpu
from jax.sharding import PartitionSpec as P

softmax_gain = 192.0 ** (-0.5)
masked_score = -1e30


def dequantize(code_values, scale_values):
    blocks = scale_values.shape[-1]
    latent_width = code_values.shape[-1]
    shaped = code_values.astype(jnp.float32).reshape(
        code_values.shape[:-1] + (blocks, latent_width // blocks)
    )
    scaled = shaped * scale_values.astype(jnp.float32)[..., None]
    return scaled.reshape(code_values.shape).astype(jnp.bfloat16)


def shard_partial(
    lat_query, rope_query, key_rows, rope_rows, usable, new_keys, new_rope_rows, holds_new
):
    tokens_new, head_count, latent_width = lat_query.shape
    query_rows = lat_query.reshape(tokens_new * head_count, latent_width)
    query_pos = rope_query.reshape(tokens_new * head_count, rope_query.shape[-1])
    scores = jnp.dot(query_rows, key_rows.T, preferred_element_type=jnp.float32)
    scores = (
        scores + jnp.dot(query_pos, rope_rows.T, preferred_element_type=jnp.float32)
    ) * softmax_gain
    fresh_scores = jnp.dot(query_rows, new_keys.T, preferred_element_type=jnp.float32)
    fresh_scores = (
        fresh_scores + jnp.dot(query_pos, new_rope_rows.T, preferred_element_type=jnp.float32)
    ) * softmax_gain
    token_of_row = jnp.arange(tokens_new * head_count, dtype=jnp.int32) // head_count
    causal = (jnp.arange(tokens_new, dtype=jnp.int32)[None, :] <= token_of_row[:, None]) & holds_new
    scores = jnp.where(usable[None, :], scores, masked_score)
    fresh_scores = jnp.where(causal, fresh_scores, masked_score)
    group_peak = jnp.maximum(jnp.max(scores, 1), jnp.max(fresh_scores, 1)).astype(jnp.bfloat16)
    peak_float = group_peak.astype(jnp.float32)[:, None]
    weights = jnp.where(usable[None, :], jnp.exp(scores - peak_float), 0.0).astype(jnp.bfloat16)
    fresh_weights = jnp.where(causal, jnp.exp(fresh_scores - peak_float), 0.0).astype(jnp.bfloat16)
    group_total = jnp.sum(weights.astype(jnp.float32), 1) + jnp.sum(
        fresh_weights.astype(jnp.float32), 1
    )
    group_sum = jnp.dot(weights, key_rows, preferred_element_type=jnp.float32)
    group_sum = group_sum + jnp.dot(fresh_weights, new_keys, preferred_element_type=jnp.float32)
    return (
        group_sum.astype(jnp.bfloat16).reshape(tokens_new, head_count, latent_width),
        group_peak.reshape(tokens_new, head_count),
        group_total.astype(jnp.bfloat16).reshape(tokens_new, head_count),
    )


def merge_groups(pieces):
    group_sum, group_peak, group_total = pieces
    peak_float = group_peak.astype(jnp.float32)
    overall = jnp.max(peak_float, 0)
    factor = jnp.exp(peak_float - overall)
    numerator = jnp.sum(factor[..., None] * group_sum.astype(jnp.float32), 0)
    denominator = jnp.sum(factor * group_total.astype(jnp.float32), 0)
    return (numerator / denominator[..., None]).astype(jnp.bfloat16)


def per_device(
    latent_codes, latent_scales, rope_keys, lengths, query_latent, query_rope, new_latent, new_rope
):
    shard_count = lax.axis_size("seq")
    seq_index = lax.axis_index("seq")
    layer_count, request_count, span, latent_width = latent_codes.shape
    lat_query, rope_query = (
        lax.all_gather(query_latent, "seq", axis=3, tiled=True),
        lax.all_gather(query_rope, "seq", axis=3, tiled=True),
    )

    def regroup_rows(values):
        return values.reshape(
            values.shape[0], values.shape[1], span // shard_count, shard_count, values.shape[-1]
        )

    codes_moved, scales_moved, rope_moved = (
        lax.all_to_all(regroup_rows(latent_codes), "seq", split_axis=3, concat_axis=2, tiled=True),
        lax.all_to_all(regroup_rows(latent_scales), "seq", split_axis=3, concat_axis=2, tiled=True),
        lax.all_to_all(regroup_rows(rope_keys), "seq", split_axis=3, concat_axis=2, tiled=True),
    )
    offsets = jnp.arange(span, dtype=jnp.int32)
    key_rows = dequantize(latent_codes, latent_scales)
    positions = seq_index * span + offsets
    usable = positions[None, :] < lengths[:, None]
    holds_new = seq_index == 0
    per_request = jax.vmap(shard_partial, in_axes=(0, 0, 0, 0, 0, 0, 0, None))
    per_layer = jax.vmap(per_request, in_axes=(0, 0, 0, 0, None, 0, 0, None))
    group_sum, group_peak, group_total = per_layer(
        lat_query, rope_query, key_rows, rope_keys, usable, new_latent, new_rope, holds_new
    )
    attended = merge_groups(
        (
            lax.all_to_all(group_sum[None], "seq", split_axis=4, concat_axis=0, tiled=True),
            lax.all_to_all(group_peak[None], "seq", split_axis=4, concat_axis=0, tiled=True),
            lax.all_to_all(group_total[None], "seq", split_axis=4, concat_axis=0, tiled=True),
        )
    )
    return (attended, codes_moved, scales_moved, rope_moved)


def _relay_kernel(
    len_ref, codes_ref, rope_ref, scale_ref, q_ref, qr_ref, new_ref, newr_ref,
    att_ref, cache_ref, crope_ref, cscale_ref,
    kbuf, abuf, raw, rawr, raws, stage, turned, qbuf, qrbuf, nkbuf, nrbuf, result, acc, peak, total,
    load_sem, out_sem, send_sem, recv_sem, q_send, q_recv, f_send, f_recv, r_send, r_recv,
):
    pairs, span, width = codes_ref.shape
    groups = 4
    rows = span // groups
    half = q_ref.shape[1]
    rope = qr_ref.shape[2]
    blocks = scale_ref.shape[1]
    heads = half // new_ref.shape[1]
    fresh = new_ref.shape[1]
    tail = groups * rope
    me = lax.axis_index("seq")
    inner = (me == 1) | (me == 2)
    outer = (me - 1) * 3
    across = 3 - me
    hub = 1 + me // 3
    side = me // 2

    def neighbour_signal(target):
        pl.semaphore_signal(
            pltpu.get_barrier_semaphore(), inc=1, device_id={"seq": target},
            device_id_type=pl.DeviceIdType.MESH,
        )

    def load(c):
        return (
            pltpu.make_async_copy(codes_ref.at[c], raw.at[c], load_sem.at[0, c]),
            pltpu.make_async_copy(rope_ref.at[c], rawr.at[c], load_sem.at[1, c]),
            pltpu.make_async_copy(scale_ref.at[c], raws.at[c], load_sem.at[2, c]),
            pltpu.make_async_copy(q_ref.at[c], qbuf.at[c, 0], load_sem.at[3, c]),
            pltpu.make_async_copy(qr_ref.at[c], qrbuf.at[c, 0], load_sem.at[4, c]),
        )

    def start(copies):
        for copy in copies:
            copy.start()

    for c in range(pairs):
        start(load(c))

    @pl.when(inner)
    def _():
        neighbour_signal(outer)
        neighbour_signal(across)

    @pl.when(jnp.logical_not(inner))
    def _():
        neighbour_signal(hub)

    def prepare_codes(c):
        for copy in load(c):
            copy.wait()
        for b in range(width // 128):
            stage[b] = raw[c, :, b * 128:(b + 1) * 128].astype(jnp.float32)
        for k in range(groups):
            for b in range(width // 128):
                kbuf[0, c, k // 2, (k % 2) * rows:(k % 2 + 1) * rows, b * 128:(b + 1) * 128] = (
                    stage[b, pl.ds(k, rows, stride=groups), :].astype(jnp.bfloat16)
                )
    def prepare_aux(c):
        turned[...] = jnp.concatenate(
            [rawr[c].astype(jnp.float32), raws[c].astype(jnp.float32),
             jnp.zeros((128 - rope - blocks, span), jnp.float32)], axis=0
        ).T
        scales = []
        for k in range(groups):
            piece = turned[pl.ds(k, rows, stride=groups), :].T
            abuf[0, c, k * rope:(k + 1) * rope, :] = piece[0:rope].astype(jnp.bfloat16)
            scales.append(piece[rope:rope + blocks])
        abuf[0, c, tail:, :] = jnp.concatenate(scales, axis=0).astype(jnp.bfloat16)

    def prepare(c):
        prepare_codes(c)
        prepare_aux(c)

    def remote(src, dst, send, recv, target):
        return pltpu.make_async_remote_copy(
            src_ref=src, dst_ref=dst, send_sem=send, recv_sem=recv,
            device_id={"seq": target}, device_id_type=pl.DeviceIdType.MESH,
        )

    def shard_aux(src, dst, c, target):
        return (
            remote(abuf.at[src, c], abuf.at[dst, c],
                   send_sem.at[1, dst, c], recv_sem.at[1, dst, c], target),
        )

    def shard_codes(src, dst, c, target, first):
        return (
            remote(kbuf.at[src, c, first], kbuf.at[dst, c, first],
                   send_sem.at[0, dst, c], recv_sem.at[0, dst, c], target),
        )

    def shard_head(src, dst, c, target, first):
        return shard_aux(src, dst, c, target) + shard_codes(src, dst, c, target, first)

    def shard_rest(src, dst, c, target, first):
        return (
            remote(kbuf.at[src, c, 1 - first], kbuf.at[dst, c, 1 - first],
                   send_sem.at[2, dst, c], recv_sem.at[2, dst, c], target),
        )

    def shard(src, dst, c, target, first):
        return shard_head(src, dst, c, target, first) + shard_rest(src, dst, c, target, first)

    def queries(c, target):
        return (
            remote(qbuf.at[c, 0], qbuf.at[c, 1], q_send.at[0, c], q_recv.at[0, c], target),
            remote(qrbuf.at[c, 0], qrbuf.at[c, 1], q_send.at[1, c], q_recv.at[1, c], target),
        )

    def shard_of(slot, own, partner):
        base = own + (slot % 2) * (partner - own)
        return base + (slot // 2) * (3 - 2 * base)

    def key_part(slot, c, group):
        return kbuf.at[slot, c, group // 2, pl.ds(pl.multiple_of((group % 2) * rows, rows), rows)]

    def rope_part(slot, c, group):
        return abuf.at[slot, c, pl.ds(pl.multiple_of(group * rope, rope), rope)]

    def cache_part(c, place):
        return cache_ref.at[c, pl.ds(pl.multiple_of(place * rows, rows), rows)]

    def crope_part(c, place):
        return crope_ref.at[c, :, pl.ds(pl.multiple_of(place * rows, rows), rows)]

    def handover(slot, c, group, place, target):
        kept = slot + 1 - jnp.minimum(slot, 1)
        return (
            remote(key_part(slot, c, group), cache_part(c, place),
                   f_send.at[0, slot, c], f_recv.at[0, slot, c], target),
            remote(rope_part(slot, c, group), crope_part(c, place),
                   f_send.at[1, slot, c], f_recv.at[1, slot, c], target),
            remote(abuf.at[slot, c, pl.ds(tail, 16)], abuf.at[kept, c, pl.ds(tail, 16)],
                   f_send.at[2, slot, c], f_recv.at[2, slot, c], target),
        )

    def keep(slot, c, place):
        return (
            pltpu.make_async_copy(key_part(slot, c, me), cache_part(c, place), out_sem.at[0, slot, c]),
            pltpu.make_async_copy(rope_part(slot, c, me), crope_part(c, place), out_sem.at[1, slot, c]),
        )

    def keep_scales(slot, c, place):
        tile = abuf[slot, c, tail:tail + 16, :].astype(jnp.float32)
        mine = tile[0:blocks]
        for k in range(1, groups):
            mine = jnp.where(me == k, tile[k * blocks:(k + 1) * blocks], mine)
        cscale_ref[c, :, pl.ds(pl.multiple_of(place * rows, rows), rows)] = mine.astype(jnp.bfloat16)

    def results(c, target):
        return remote(result.at[c], att_ref.at[c], r_send.at[c], r_recv.at[c], target)

    prepare_codes(0)

    @pl.when(jnp.logical_not(inner))
    def _():
        pl.semaphore_wait(pltpu.get_barrier_semaphore(), 1)

        prepare_aux(0)

        @pl.loop(0, pairs)
        def _(c):
            copies = shard(0, 1, c, hub, side) + queries(c, hub)
            start(copies)
            start(keep(0, c, me))
            keep_scales(0, c, me)

            @pl.when(c + 1 < pairs)
            def _():
                prepare(c + 1)

            for copy in copies:
                copy.wait_send()

        @pl.loop(0, pairs)
        def _(c):
            for slot in (0, 2, 3):
                place = shard_of(slot, hub, me)
                for copy in handover(slot, c, me, place, hub):
                    copy.wait_recv()
                keep_scales(max(slot, 1), c, place)
            results(c, hub).wait_recv()
            for copy in keep(0, c, me):
                copy.wait()

    @pl.when(inner)
    def _():
        pl.semaphore_wait(pltpu.get_barrier_semaphore(), 2)
        start(shard_codes(0, 2, 0, across, 1 - side) + shard_rest(0, 2, 0, across, 1 - side))
        prepare_aux(0)
        start(shard_aux(0, 2, 0, across))

        @pl.loop(0, pairs)
        def _(c):
            @pl.when(c == 1)
            def _():
                start(shard(0, 2, c, across, 1 - side))

            start(handover(0, c, outer, me, outer))
            start(keep(0, c, me))
            keep_scales(0, c, me)
            nkbuf[c] = jnp.zeros(nkbuf.shape[1:], nkbuf.dtype)
            nrbuf[c] = jnp.zeros(nrbuf.shape[1:], nrbuf.dtype)
            nkbuf[c, 0:fresh, :] = new_ref[c]
            nrbuf[c, 0:fresh, :] = newr_ref[c]

            @pl.when(c + 1 < pairs)
            def _():
                prepare(c + 1)

        def relay(c):
            for copy in shard(0, 1, c, outer, side):
                copy.wait_recv()
            start(shard(1, 3, c, across, 1 - side))
            start(keep(1, c, outer))

        relay(0)
        start(shard(0, 2, 2, across, 1 - side))

        @pl.loop(0, pairs)
        def _(c):
            @pl.when(c + 1 < pairs)
            def _():
                relay(c + 1)

            @pl.when(c + 3 < pairs)
            def _():
                start(shard(0, 2, c + 3, across, 1 - side))

            for copy in queries(c, outer):
                copy.wait_recv()
            q = qbuf[c].reshape(2 * half, width)
            qr = qrbuf[c].reshape(2 * half, rope)
            dims = (((1,), (1,)), ((), ()))
            s = lax.dot_general(q, nkbuf[c], dims, preferred_element_type=jnp.float32)
            s = s + lax.dot_general(qr, nrbuf[c], dims, preferred_element_type=jnp.float32)
            s = s * softmax_gain
            token = (lax.broadcasted_iota(jnp.int32, s.shape, 0) % half) // heads
            s = jnp.where(lax.broadcasted_iota(jnp.int32, s.shape, 1) <= token, s, masked_score)
            m = jnp.max(s, axis=1, keepdims=True)
            w = jnp.exp(s - m).astype(jnp.bfloat16)
            peak[...] = jnp.broadcast_to(m, peak.shape)
            total[...] = jnp.broadcast_to(
                jnp.sum(w.astype(jnp.float32), axis=1, keepdims=True), total.shape
            )
            acc[...] = jnp.dot(w, nkbuf[c], preferred_element_type=jnp.float32)
            length = len_ref[c % len_ref.shape[0]]

            @pl.loop(0, 8)
            def _(step):
                slot = step // 2
                part = side + (step % 2) * (1 - 2 * side)
                place = shard_of(slot, me, outer)

                @pl.when((slot >= 2) & (step % 2 == 0))
                def _():
                    for copy in shard_head(0, slot, c, across, side):
                        copy.wait_recv()
                    start(handover(slot, c, outer, place, outer))
                    start(keep(slot, c, place))

                @pl.when((slot >= 2) & (step % 2 == 1))
                def _():
                    for copy in shard_rest(0, slot, c, across, side):
                        copy.wait_recv()

                @pl.when((slot >= 1) & (step % 2 == 0))
                def _():
                    keep_scales(slot, c, place)

                scales = abuf[slot, c, tail:tail + 16, :].astype(jnp.float32)
                scales = jnp.where(side + step % 2 == 1, scales[8:16], scales[0:8]).T
                keys = []
                for k in range(2):
                    codes = kbuf[slot, c, part, k * rows:(k + 1) * rows, :].astype(jnp.float32)
                    keys.append(jnp.concatenate([
                        codes[:, b * 128:(b + 1) * 128] * scales[:, k * blocks + b:k * blocks + b + 1]
                        for b in range(blocks)
                    ], axis=1).astype(jnp.bfloat16))
                keys = jnp.concatenate(keys, axis=0)
                base = pl.multiple_of(part * 2 * rope, 2 * rope)
                ropes = jnp.concatenate(
                    [abuf[slot, c, pl.ds(base, rope), :], abuf[slot, c, pl.ds(base + rope, rope), :]],
                    axis=1,
                )
                q = qbuf[c].reshape(2 * half, width)
                qr = qrbuf[c].reshape(2 * half, rope)
                s = lax.dot_general(q, keys, dims, preferred_element_type=jnp.float32)
                s = s + jnp.dot(qr, ropes, preferred_element_type=jnp.float32)
                s = s * softmax_gain
                column = lax.broadcasted_iota(jnp.int32, (1, 2 * rows), 1)
                position = place * span + (column % rows) * groups + 2 * part + column // rows
                s = jnp.where(position < length, s, masked_score)
                before = peak[:, 0:1]
                m = jnp.maximum(before, jnp.max(s, axis=1, keepdims=True))
                factor = jnp.exp(before - m)
                w = jnp.exp(s - m).astype(jnp.bfloat16)
                peak[...] = jnp.broadcast_to(m, peak.shape)
                total[...] = factor * total[...] + jnp.sum(w.astype(jnp.float32), axis=1, keepdims=True)
                acc[...] = factor * acc[...] + jnp.dot(w, keys, preferred_element_type=jnp.float32)

            result[c] = (acc[half:, :] / total[half:, 0:1]).astype(jnp.bfloat16)
            results(c, outer).start()
            att_ref[c] = (acc[:half, :] / total[:half, 0:1]).astype(jnp.bfloat16)

        @pl.loop(0, pairs)
        def _(c):
            for copy in shard(0, 2, c, across, 1 - side) + shard(1, 3, c, across, 1 - side):
                copy.wait_send()
            for slot in (0, 2, 3):
                for copy in handover(slot, c, outer, shard_of(slot, me, outer), outer):
                    copy.wait_send()
            for slot in range(4):
                for copy in keep(slot, c, shard_of(slot, me, outer)):
                    copy.wait()
            results(c, outer).wait_send()


def per_device_line(
    latent_codes, latent_scales, rope_keys, lengths, query_latent, query_rope, new_latent, new_rope
):
    layers, requests, span, width = latent_codes.shape
    pairs, rows = layers * requests, span // 4
    rope, blocks = rope_keys.shape[-1], latent_scales.shape[-1]
    tokens, heads = query_latent.shape[2:4]
    half = tokens * heads
    aux = 4 * rope + 16
    hbm_spec = pl.BlockSpec(memory_space=pltpu.HBM)
    any_spec = pl.BlockSpec(memory_space=pl.ANY)
    vmem_spec = pl.BlockSpec(memory_space=pltpu.VMEM)
    dma = pltpu.SemaphoreType.DMA
    bf16, f32 = jnp.bfloat16, jnp.float32
    att, cache, crope, cscale = pl.pallas_call(
        _relay_kernel,
        out_shape=(
            jax.ShapeDtypeStruct((pairs, half, width), bf16),
            jax.ShapeDtypeStruct((pairs, span, width), bf16),
            jax.ShapeDtypeStruct((pairs, rope, span), bf16),
            jax.ShapeDtypeStruct((pairs, blocks, span), bf16),
        ),
        in_specs=[pl.BlockSpec(memory_space=pltpu.SMEM)] + [hbm_spec] * 5 + [vmem_spec] * 2,
        out_specs=(vmem_spec, any_spec, any_spec, vmem_spec),
        scratch_shapes=[
            pltpu.VMEM((4, pairs, 2, 2 * rows, width), bf16),
            pltpu.VMEM((4, pairs, aux, rows), bf16),
            pltpu.VMEM((pairs, span, width), bf16),
            pltpu.VMEM((pairs, rope, span), bf16),
            pltpu.VMEM((pairs, blocks, span), bf16),
            pltpu.VMEM((width // 128, span, 128), f32),
            pltpu.VMEM((span, 128), f32),
            pltpu.VMEM((pairs, 2, half, width), bf16),
            pltpu.VMEM((pairs, 2, half, rope), bf16),
            pltpu.VMEM((pairs, 128, width), bf16),
            pltpu.VMEM((pairs, 128, rope), bf16),
            pltpu.VMEM((pairs, half, width), bf16),
            pltpu.VMEM((2 * half, width), f32),
            pltpu.VMEM((2 * half, 128), f32),
            pltpu.VMEM((2 * half, 128), f32),
            dma((5, pairs)), dma((2, 4, pairs)), dma((3, 4, pairs)), dma((3, 4, pairs)),
            dma((2, pairs)), dma((2, pairs)), dma((3, 4, pairs)), dma((3, 4, pairs)),
            dma((pairs,)), dma((pairs,)),
        ],
        compiler_params=pltpu.CompilerParams(
            collective_id=0, has_side_effects=True, vmem_limit_bytes=60 << 20
        ),
    )(
        lengths, latent_codes.reshape(pairs, span, width),
        rope_keys.transpose(0, 1, 3, 2).reshape(pairs, rope, span),
        latent_scales.transpose(0, 1, 3, 2).reshape(pairs, blocks, span),
        query_latent.reshape(pairs, half, width), query_rope.reshape(pairs, half, rope),
        new_latent.reshape(pairs, tokens, width), new_rope.reshape(pairs, tokens, rope),
    )

    def as_cache(values):
        flipped = values.reshape(layers, requests, values.shape[1], span).transpose(0, 1, 3, 2)
        return flipped.reshape(layers, requests, span, 1, values.shape[1])

    return (
        att.reshape(query_latent.shape),
        cache.reshape(layers, requests, span, 1, width),
        as_cache(cscale),
        as_cache(crope),
    )


def solution(mesh):
    placed = (
        P(None, ("group", "req", "sub"), "seq", None),
        P(None, ("group", "req", "sub"), "seq", None),
        P(None, ("group", "req", "sub"), "seq", None),
        P(("group", "req", "sub")),
        P(None, ("group", "req", "sub"), None, "seq", None),
        P(None, ("group", "req", "sub"), None, "seq", None),
        P(None, ("group", "req", "sub"), None, None),
        P(None, ("group", "req", "sub"), None, None),
    )
    return jax.shard_map(
        per_device_line if mesh.shape["seq"] == 4 else per_device,
        mesh=mesh,
        in_specs=placed,
        out_specs=(
            P(None, ("group", "req", "sub"), None, "seq", None),
            P(None, ("group", "req", "sub"), None, "seq", None),
            P(None, ("group", "req", "sub"), None, "seq", None),
            P(None, ("group", "req", "sub"), None, "seq", None),
        ),
        check_vma=False,
    )
```

```python
import jax
import jax.numpy as jnp
from jax import lax
from jax.experimental import pallas as pl
from jax.experimental.pallas import tpu as pltpu
from jax.sharding import PartitionSpec as P

softmax_gain = 192.0 ** (-0.5)
masked_score = -1e30


def dequantize(code_values, scale_values):
    blocks = scale_values.shape[-1]
    latent_width = code_values.shape[-1]
    shaped = code_values.astype(jnp.float32).reshape(
        code_values.shape[:-1] + (blocks, latent_width // blocks)
    )
    scaled = shaped * scale_values.astype(jnp.float32)[..., None]
    return scaled.reshape(code_values.shape).astype(jnp.bfloat16)


def shard_partial(
    lat_query, rope_query, key_rows, rope_rows, usable, new_keys, new_rope_rows, holds_new
):
    tokens_new, head_count, latent_width = lat_query.shape
    query_rows = lat_query.reshape(tokens_new * head_count, latent_width)
    query_pos = rope_query.reshape(tokens_new * head_count, rope_query.shape[-1])
    scores = jnp.dot(query_rows, key_rows.T, preferred_element_type=jnp.float32)
    scores = (
        scores + jnp.dot(query_pos, rope_rows.T, preferred_element_type=jnp.float32)
    ) * softmax_gain
    fresh_scores = jnp.dot(query_rows, new_keys.T, preferred_element_type=jnp.float32)
    fresh_scores = (
        fresh_scores + jnp.dot(query_pos, new_rope_rows.T, preferred_element_type=jnp.float32)
    ) * softmax_gain
    token_of_row = jnp.arange(tokens_new * head_count, dtype=jnp.int32) // head_count
    causal = (jnp.arange(tokens_new, dtype=jnp.int32)[None, :] <= token_of_row[:, None]) & holds_new
    scores = jnp.where(usable[None, :], scores, masked_score)
    fresh_scores = jnp.where(causal, fresh_scores, masked_score)
    group_peak = jnp.maximum(jnp.max(scores, 1), jnp.max(fresh_scores, 1)).astype(jnp.bfloat16)
    peak_float = group_peak.astype(jnp.float32)[:, None]
    weights = jnp.where(usable[None, :], jnp.exp(scores - peak_float), 0.0).astype(jnp.bfloat16)
    fresh_weights = jnp.where(causal, jnp.exp(fresh_scores - peak_float), 0.0).astype(jnp.bfloat16)
    group_total = jnp.sum(weights.astype(jnp.float32), 1) + jnp.sum(
        fresh_weights.astype(jnp.float32), 1
    )
    group_sum = jnp.dot(weights, key_rows, preferred_element_type=jnp.float32)
    group_sum = group_sum + jnp.dot(fresh_weights, new_keys, preferred_element_type=jnp.float32)
    return (
        group_sum.astype(jnp.bfloat16).reshape(tokens_new, head_count, latent_width),
        group_peak.reshape(tokens_new, head_count),
        group_total.astype(jnp.bfloat16).reshape(tokens_new, head_count),
    )


def merge_groups(pieces):
    group_sum, group_peak, group_total = pieces
    peak_float = group_peak.astype(jnp.float32)
    overall = jnp.max(peak_float, 0)
    factor = jnp.exp(peak_float - overall)
    numerator = jnp.sum(factor[..., None] * group_sum.astype(jnp.float32), 0)
    denominator = jnp.sum(factor * group_total.astype(jnp.float32), 0)
    return (numerator / denominator[..., None]).astype(jnp.bfloat16)


def per_device(
    latent_codes, latent_scales, rope_keys, lengths, query_latent, query_rope, new_latent, new_rope
):
    shard_count = lax.axis_size("seq")
    seq_index = lax.axis_index("seq")
    layer_count, request_count, span, latent_width = latent_codes.shape
    lat_query, rope_query = (
        lax.all_gather(query_latent, "seq", axis=3, tiled=True),
        lax.all_gather(query_rope, "seq", axis=3, tiled=True),
    )

    def regroup_rows(values):
        return values.reshape(
            values.shape[0], values.shape[1], span // shard_count, shard_count, values.shape[-1]
        )

    codes_moved, scales_moved, rope_moved = (
        lax.all_to_all(regroup_rows(latent_codes), "seq", split_axis=3, concat_axis=2, tiled=True),
        lax.all_to_all(regroup_rows(latent_scales), "seq", split_axis=3, concat_axis=2, tiled=True),
        lax.all_to_all(regroup_rows(rope_keys), "seq", split_axis=3, concat_axis=2, tiled=True),
    )
    offsets = jnp.arange(span, dtype=jnp.int32)
    key_rows = dequantize(latent_codes, latent_scales)
    positions = seq_index * span + offsets
    usable = positions[None, :] < lengths[:, None]
    holds_new = seq_index == 0
    per_request = jax.vmap(shard_partial, in_axes=(0, 0, 0, 0, 0, 0, 0, None))
    per_layer = jax.vmap(per_request, in_axes=(0, 0, 0, 0, None, 0, 0, None))
    group_sum, group_peak, group_total = per_layer(
        lat_query, rope_query, key_rows, rope_keys, usable, new_latent, new_rope, holds_new
    )
    attended = merge_groups(
        (
            lax.all_to_all(group_sum[None], "seq", split_axis=4, concat_axis=0, tiled=True),
            lax.all_to_all(group_peak[None], "seq", split_axis=4, concat_axis=0, tiled=True),
            lax.all_to_all(group_total[None], "seq", split_axis=4, concat_axis=0, tiled=True),
        )
    )
    return (attended, codes_moved, scales_moved, rope_moved)


def _relay_kernel(
    len_ref, codes_ref, rope_ref, scale_ref, q_ref, qr_ref, new_ref, newr_ref,
    att_ref, cache_ref, crope_ref, cscale_ref,
    kbuf, abuf, raw, rawr, raws, stage, turned, qbuf, qrbuf, nkbuf, nrbuf, result, acc, peak, total,
    load_sem, out_sem, send_sem, recv_sem, q_send, q_recv, f_send, f_recv, r_send, r_recv,
):
    pairs, span, width = codes_ref.shape
    groups = 4
    rows = span // groups
    half = q_ref.shape[1]
    rope = qr_ref.shape[2]
    blocks = scale_ref.shape[1]
    heads = half // new_ref.shape[1]
    fresh = new_ref.shape[1]
    tail = groups * rope
    me = lax.axis_index("seq")
    inner = (me == 1) | (me == 2)
    outer = (me - 1) * 3
    across = 3 - me
    hub = 1 + me // 3
    side = me // 2

    def neighbour_signal(target):
        pl.semaphore_signal(
            pltpu.get_barrier_semaphore(), inc=1, device_id={"seq": target},
            device_id_type=pl.DeviceIdType.MESH,
        )

    def load(c):
        return (
            pltpu.make_async_copy(codes_ref.at[c], raw.at[c], load_sem.at[0, c]),
            pltpu.make_async_copy(rope_ref.at[c], rawr.at[c], load_sem.at[1, c]),
            pltpu.make_async_copy(scale_ref.at[c], raws.at[c], load_sem.at[2, c]),
            pltpu.make_async_copy(q_ref.at[c], qbuf.at[c, 0], load_sem.at[3, c]),
            pltpu.make_async_copy(qr_ref.at[c], qrbuf.at[c, 0], load_sem.at[4, c]),
        )

    def start(copies):
        for copy in copies:
            copy.start()

    for c in range(pairs):
        start(load(c))

    @pl.when(inner)
    def _():
        neighbour_signal(outer)
        neighbour_signal(across)

    @pl.when(jnp.logical_not(inner))
    def _():
        neighbour_signal(hub)

    def prepare_codes(c):
        for copy in load(c):
            copy.wait()
        for b in range(width // 128):
            stage[b] = raw[c, :, b * 128:(b + 1) * 128].astype(jnp.float32)
        for k in range(groups):
            for b in range(width // 128):
                kbuf[0, c, k // 2, (k % 2) * rows:(k % 2 + 1) * rows, b * 128:(b + 1) * 128] = (
                    stage[b, pl.ds(k, rows, stride=groups), :].astype(jnp.bfloat16)
                )
    def prepare_aux(c):
        turned[...] = jnp.concatenate(
            [rawr[c].astype(jnp.float32), raws[c].astype(jnp.float32),
             jnp.zeros((128 - rope - blocks, span), jnp.float32)], axis=0
        ).T
        scales = []
        for k in range(groups):
            piece = turned[pl.ds(k, rows, stride=groups), :].T
            abuf[0, c, k * rope:(k + 1) * rope, :] = piece[0:rope].astype(jnp.bfloat16)
            scales.append(piece[rope:rope + blocks])
        abuf[0, c, tail:, :] = jnp.concatenate(scales, axis=0).astype(jnp.bfloat16)

    def prepare(c):
        prepare_codes(c)
        prepare_aux(c)

    def remote(src, dst, send, recv, target):
        return pltpu.make_async_remote_copy(
            src_ref=src, dst_ref=dst, send_sem=send, recv_sem=recv,
            device_id={"seq": target}, device_id_type=pl.DeviceIdType.MESH,
        )

    def shard_aux(src, dst, c, target):
        return (
            remote(abuf.at[src, c], abuf.at[dst, c],
                   send_sem.at[1, dst, c], recv_sem.at[1, dst, c], target),
        )

    def shard_codes(src, dst, c, target, first):
        return (
            remote(kbuf.at[src, c, first], kbuf.at[dst, c, first],
                   send_sem.at[0, dst, c], recv_sem.at[0, dst, c], target),
        )

    def shard_head(src, dst, c, target, first):
        return shard_aux(src, dst, c, target) + shard_codes(src, dst, c, target, first)

    def shard_rest(src, dst, c, target, first):
        return (
            remote(kbuf.at[src, c, 1 - first], kbuf.at[dst, c, 1 - first],
                   send_sem.at[2, dst, c], recv_sem.at[2, dst, c], target),
        )

    def shard(src, dst, c, target, first):
        return shard_head(src, dst, c, target, first) + shard_rest(src, dst, c, target, first)

    def queries(c, target):
        return (
            remote(qbuf.at[c, 0], qbuf.at[c, 1], q_send.at[0, c], q_recv.at[0, c], target),
            remote(qrbuf.at[c, 0], qrbuf.at[c, 1], q_send.at[1, c], q_recv.at[1, c], target),
        )

    def shard_of(slot, own, partner):
        base = own + (slot % 2) * (partner - own)
        return base + (slot // 2) * (3 - 2 * base)

    def key_part(slot, c, group):
        return kbuf.at[slot, c, group // 2, pl.ds(pl.multiple_of((group % 2) * rows, rows), rows)]

    def rope_part(slot, c, group):
        return abuf.at[slot, c, pl.ds(pl.multiple_of(group * rope, rope), rope)]

    def cache_part(c, place):
        return cache_ref.at[c, pl.ds(pl.multiple_of(place * rows, rows), rows)]

    def crope_part(c, place):
        return crope_ref.at[c, :, pl.ds(pl.multiple_of(place * rows, rows), rows)]

    def handover(slot, c, group, place, target):
        kept = slot + 1 - jnp.minimum(slot, 1)
        return (
            remote(key_part(slot, c, group), cache_part(c, place),
                   f_send.at[0, slot, c], f_recv.at[0, slot, c], target),
            remote(rope_part(slot, c, group), crope_part(c, place),
                   f_send.at[1, slot, c], f_recv.at[1, slot, c], target),
            remote(abuf.at[slot, c, pl.ds(tail, 16)], abuf.at[kept, c, pl.ds(tail, 16)],
                   f_send.at[2, slot, c], f_recv.at[2, slot, c], target),
        )

    def keep(slot, c, place):
        return (
            pltpu.make_async_copy(key_part(slot, c, me), cache_part(c, place), out_sem.at[0, slot, c]),
            pltpu.make_async_copy(rope_part(slot, c, me), crope_part(c, place), out_sem.at[1, slot, c]),
        )

    def keep_scales(slot, c, place):
        tile = abuf[slot, c, tail:tail + 16, :].astype(jnp.float32)
        mine = tile[0:blocks]
        for k in range(1, groups):
            mine = jnp.where(me == k, tile[k * blocks:(k + 1) * blocks], mine)
        cscale_ref[c, :, pl.ds(pl.multiple_of(place * rows, rows), rows)] = mine.astype(jnp.bfloat16)

    def results(c, target):
        return remote(result.at[c, 1], att_ref.at[c], r_send.at[c], r_recv.at[c], target)

    def own_results(c):
        return pltpu.make_async_copy(result.at[c, 0], att_ref.at[c], load_sem.at[5, c])

    prepare_codes(0)

    @pl.when(jnp.logical_not(inner))
    def _():
        pl.semaphore_wait(pltpu.get_barrier_semaphore(), 1)

        prepare_aux(0)

        @pl.loop(0, pairs)
        def _(c):
            copies = shard(0, 1, c, hub, side) + queries(c, hub)
            start(copies)
            start(keep(0, c, me))
            keep_scales(0, c, me)

            @pl.when(c + 1 < pairs)
            def _():
                prepare(c + 1)

            for copy in copies:
                copy.wait_send()

        @pl.loop(0, pairs)
        def _(c):
            for slot in (0, 2, 3):
                place = shard_of(slot, hub, me)
                for copy in handover(slot, c, me, place, hub):
                    copy.wait_recv()
                keep_scales(max(slot, 1), c, place)
            results(c, hub).wait_recv()
            for copy in keep(0, c, me):
                copy.wait()

    @pl.when(inner)
    def _():
        pl.semaphore_wait(pltpu.get_barrier_semaphore(), 2)
        start(shard_codes(0, 2, 0, across, 1 - side) + shard_rest(0, 2, 0, across, 1 - side))
        prepare_aux(0)
        start(shard_aux(0, 2, 0, across))

        @pl.loop(0, pairs)
        def _(c):
            @pl.when(c == 1)
            def _():
                start(shard(0, 2, c, across, 1 - side))

            start(handover(0, c, outer, me, outer))
            start(keep(0, c, me))
            keep_scales(0, c, me)
            nkbuf[c] = jnp.zeros(nkbuf.shape[1:], nkbuf.dtype)
            nrbuf[c] = jnp.zeros(nrbuf.shape[1:], nrbuf.dtype)
            nkbuf[c, 0:fresh, :] = new_ref[c]
            nrbuf[c, 0:fresh, :] = newr_ref[c]

            @pl.when(c + 1 < pairs)
            def _():
                prepare(c + 1)

        def relay(c):
            for copy in shard(0, 1, c, outer, side):
                copy.wait_recv()
            start(shard(1, 3, c, across, 1 - side))
            start(keep(1, c, outer))

        relay(0)
        start(shard(0, 2, 2, across, 1 - side))

        @pl.loop(0, pairs)
        def _(c):
            @pl.when(c + 1 < pairs)
            def _():
                relay(c + 1)

            @pl.when(c + 3 < pairs)
            def _():
                start(shard(0, 2, c + 3, across, 1 - side))

            for copy in queries(c, outer):
                copy.wait_recv()
            q = qbuf[c].reshape(2 * half, width)
            qr = qrbuf[c].reshape(2 * half, rope)
            dims = (((1,), (1,)), ((), ()))
            s = lax.dot_general(q, nkbuf[c], dims, preferred_element_type=jnp.float32)
            s = s + lax.dot_general(qr, nrbuf[c], dims, preferred_element_type=jnp.float32)
            s = s * softmax_gain
            token = (lax.broadcasted_iota(jnp.int32, s.shape, 0) % half) // heads
            s = jnp.where(lax.broadcasted_iota(jnp.int32, s.shape, 1) <= token, s, masked_score)
            m = jnp.max(s, axis=1, keepdims=True)
            w = jnp.exp(s - m).astype(jnp.bfloat16)
            peak[...] = jnp.broadcast_to(m, peak.shape)
            total[...] = jnp.broadcast_to(
                jnp.sum(w.astype(jnp.float32), axis=1, keepdims=True), total.shape
            )
            acc[...] = jnp.dot(w, nkbuf[c], preferred_element_type=jnp.float32)
            length = len_ref[c % len_ref.shape[0]]

            @pl.loop(0, 8)
            def _(step):
                slot = step // 2
                part = side + (step % 2) * (1 - 2 * side)
                place = shard_of(slot, me, outer)

                @pl.when((slot >= 2) & (step % 2 == 0))
                def _():
                    for copy in shard_head(0, slot, c, across, side):
                        copy.wait_recv()
                    start(handover(slot, c, outer, place, outer))
                    start(keep(slot, c, place))

                @pl.when((slot >= 2) & (step % 2 == 1))
                def _():
                    for copy in shard_rest(0, slot, c, across, side):
                        copy.wait_recv()

                @pl.when((slot >= 1) & (step % 2 == 0))
                def _():
                    keep_scales(slot, c, place)

                scales = abuf[slot, c, tail:tail + 16, :].astype(jnp.float32)
                scales = jnp.where(side + step % 2 == 1, scales[8:16], scales[0:8]).T
                keys = []
                for k in range(2):
                    codes = kbuf[slot, c, part, k * rows:(k + 1) * rows, :].astype(jnp.float32)
                    keys.append(jnp.concatenate([
                        codes[:, b * 128:(b + 1) * 128] * scales[:, k * blocks + b:k * blocks + b + 1]
                        for b in range(blocks)
                    ], axis=1).astype(jnp.bfloat16))
                keys = jnp.concatenate(keys, axis=0)
                base = pl.multiple_of(part * 2 * rope, 2 * rope)
                ropes = jnp.concatenate(
                    [abuf[slot, c, pl.ds(base, rope), :], abuf[slot, c, pl.ds(base + rope, rope), :]],
                    axis=1,
                )
                q = qbuf[c].reshape(2 * half, width)
                qr = qrbuf[c].reshape(2 * half, rope)
                s = lax.dot_general(q, keys, dims, preferred_element_type=jnp.float32)
                s = s + jnp.dot(qr, ropes, preferred_element_type=jnp.float32)
                s = s * softmax_gain
                column = lax.broadcasted_iota(jnp.int32, (1, 2 * rows), 1)
                position = place * span + (column % rows) * groups + 2 * part + column // rows
                s = jnp.where(position < length, s, masked_score)
                before = peak[:, 0:1]
                m = jnp.maximum(before, jnp.max(s, axis=1, keepdims=True))
                factor = jnp.exp(before - m)
                w = jnp.exp(s - m).astype(jnp.bfloat16)
                peak[...] = jnp.broadcast_to(m, peak.shape)
                total[...] = factor * total[...] + jnp.sum(w.astype(jnp.float32), axis=1, keepdims=True)
                acc[...] = factor * acc[...] + jnp.dot(w, keys, preferred_element_type=jnp.float32)

            result[c, 1] = (acc[half:, :] / total[half:, 0:1]).astype(jnp.bfloat16)
            results(c, outer).start()
            result[c, 0] = (acc[:half, :] / total[:half, 0:1]).astype(jnp.bfloat16)
            own_results(c).start()

        @pl.loop(0, pairs)
        def _(c):
            for copy in shard(0, 2, c, across, 1 - side) + shard(1, 3, c, across, 1 - side):
                copy.wait_send()
            for slot in (0, 2, 3):
                for copy in handover(slot, c, outer, shard_of(slot, me, outer), outer):
                    copy.wait_send()
            for slot in range(4):
                for copy in keep(slot, c, shard_of(slot, me, outer)):
                    copy.wait()
            results(c, outer).wait_send()
            own_results(c).wait()


def per_device_line(
    latent_codes, latent_scales, rope_keys, lengths, query_latent, query_rope, new_latent, new_rope
):
    layers, requests, span, width = latent_codes.shape
    pairs, rows = layers * requests, span // 4
    rope, blocks = rope_keys.shape[-1], latent_scales.shape[-1]
    tokens, heads = query_latent.shape[2:4]
    half = tokens * heads
    aux = 4 * rope + 16
    hbm_spec = pl.BlockSpec(memory_space=pltpu.HBM)
    any_spec = pl.BlockSpec(memory_space=pl.ANY)
    vmem_spec = pl.BlockSpec(memory_space=pltpu.VMEM)
    dma = pltpu.SemaphoreType.DMA
    bf16, f32 = jnp.bfloat16, jnp.float32
    att, cache, crope, cscale = pl.pallas_call(
        _relay_kernel,
        out_shape=(
            jax.ShapeDtypeStruct((pairs, half, width), bf16),
            jax.ShapeDtypeStruct((pairs, span, width), bf16),
            jax.ShapeDtypeStruct((pairs, rope, span), bf16),
            jax.ShapeDtypeStruct((pairs, blocks, span), bf16),
        ),
        in_specs=[pl.BlockSpec(memory_space=pltpu.SMEM)] + [hbm_spec] * 5 + [vmem_spec] * 2,
        out_specs=(any_spec, any_spec, any_spec, vmem_spec),
        scratch_shapes=[
            pltpu.VMEM((4, pairs, 2, 2 * rows, width), bf16),
            pltpu.VMEM((4, pairs, aux, rows), bf16),
            pltpu.VMEM((pairs, span, width), bf16),
            pltpu.VMEM((pairs, rope, span), bf16),
            pltpu.VMEM((pairs, blocks, span), bf16),
            pltpu.VMEM((width // 128, span, 128), f32),
            pltpu.VMEM((span, 128), f32),
            pltpu.VMEM((pairs, 2, half, width), bf16),
            pltpu.VMEM((pairs, 2, half, rope), bf16),
            pltpu.VMEM((pairs, 128, width), bf16),
            pltpu.VMEM((pairs, 128, rope), bf16),
            pltpu.VMEM((pairs, 2, half, width), bf16),
            pltpu.VMEM((2 * half, width), f32),
            pltpu.VMEM((2 * half, 128), f32),
            pltpu.VMEM((2 * half, 128), f32),
            dma((6, pairs)), dma((2, 4, pairs)), dma((3, 4, pairs)), dma((3, 4, pairs)),
            dma((2, pairs)), dma((2, pairs)), dma((3, 4, pairs)), dma((3, 4, pairs)),
            dma((pairs,)), dma((pairs,)),
        ],
        compiler_params=pltpu.CompilerParams(
            collective_id=0, has_side_effects=True, vmem_limit_bytes=60 << 20
        ),
    )(
        lengths, latent_codes.reshape(pairs, span, width),
        rope_keys.transpose(0, 1, 3, 2).reshape(pairs, rope, span),
        latent_scales.transpose(0, 1, 3, 2).reshape(pairs, blocks, span),
        query_latent.reshape(pairs, half, width), query_rope.reshape(pairs, half, rope),
        new_latent.reshape(pairs, tokens, width), new_rope.reshape(pairs, tokens, rope),
    )

    def as_cache(values):
        flipped = values.reshape(layers, requests, values.shape[1], span).transpose(0, 1, 3, 2)
        return flipped.reshape(layers, requests, span, 1, values.shape[1])

    return (
        att.reshape(query_latent.shape),
        cache.reshape(layers, requests, span, 1, width),
        as_cache(cscale),
        as_cache(crope),
    )


def solution(mesh):
    placed = (
        P(None, ("group", "req", "sub"), "seq", None),
        P(None, ("group", "req", "sub"), "seq", None),
        P(None, ("group", "req", "sub"), "seq", None),
        P(("group", "req", "sub")),
        P(None, ("group", "req", "sub"), None, "seq", None),
        P(None, ("group", "req", "sub"), None, "seq", None),
        P(None, ("group", "req", "sub"), None, None),
        P(None, ("group", "req", "sub"), None, None),
    )
    return jax.shard_map(
        per_device_line if mesh.shape["seq"] == 4 else per_device,
        mesh=mesh,
        in_specs=placed,
        out_specs=(
            P(None, ("group", "req", "sub"), None, "seq", None),
            P(None, ("group", "req", "sub"), None, "seq", None),
            P(None, ("group", "req", "sub"), None, "seq", None),
            P(None, ("group", "req", "sub"), None, "seq", None),
        ),
        check_vma=False,
    )
```
